32 devices in a mesh: lat: 8 (over z, x), lon: 4 (over y, core).
Axes of the slice: x: 2, y: 2, z: 4, core: 2. Of those that a mesh axis runs over, the one named last changes fastest.
Arguments:
- state_init: float32 [16, 65536], P(None, ('lat', 'lon')), may hold values from -6 to 6
- tangent_init: float32 [16, 65536], P(None, ('lat', 'lon')), may hold values from -6 to 6
- coef_blocks: bfloat16 [512, 6, 128, 128], P(('lat', 'lon')), may hold values from -0.21875 to 0.21875
- column_lists: int32 [512, 6], P(('lat', 'lon')), may hold values from 0 to 24, as said below
- send_lists: int32 [32, 4, 2], P(('lat', 'lon')), may hold values from 0 to 15, as said below
- implicit_blocks: bfloat16 [512, 128, 128], P(('lat', 'lon')), may hold values from -0.5 to 0.5
- uptake_rate: float32 [65536], P(('lat', 'lon')), may hold values from 0.5 to 4
- coupling: float32 [16, 16], replicated, may hold values from -1.5 to 1.5
- region_map: int32 [65536], P(('lat', 'lon')), may hold values from 0 to 255, as said below
- coarse_inverse: float32 [256, 256], P(('lat', 'lon')), may hold values from -0.0234375 to 0.0234375
Outputs:
- final_state: float32 [16, 65536], P(None, ('lat', 'lon'))
- preconditioned: float32 [16, 65536], P(None, ('lat', 'lon'))
The draws below stay inside these ranges and needn't reach their ends.
Inputs may be any that keep to these rules, and one draw needn't show every extreme that they name: `column_lists`: entry 0 of row block b's list is b's own index within its tile; entries 1 to 4 lie in the blocks from the lower lat, higher lat, lower lon and higher lon neighbours in that order; the rest are own blocks or 24, the zero block. `send_lists`: indices of the sending tile's own row blocks. `region_map`: region c is owned by tile c // 8; a row's region is owned by its own tile or by one of its two lon neighbours (wrapping).
All inputs are finite; a program needn't handle non-finite values.
Results may differ from the reference program's by a relative error of at most 0.0064.
Values may be sent and summed in bfloat16 or wider, within the bound.
No kernel may reach another device: no remote copies, remote signals or barrier semaphores. Data moves between devices by JAX's collectives and lax.ppermute only.
A program may use at most 64 MiB of HBM per device.

```python
import math
import jax
import jax.numpy as jnp
from jax import lax

NT = 16
BLOCK = 128
RB = 16
K = 6
HB = 2
STEPS = 2
REG_DEV = 8
ROWS = 65536
BLOCKS = 512
NC = 256
N_LAT = 8
N_LON = 4


def draw_column_lists(key, part):
    block_ids = jnp.arange(BLOCKS, dtype=jnp.int32) % RB
    offset = jax.random.randint(jax.random.fold_in(key, 11), (BLOCKS, 1), 0, HB)
    sides = RB + jnp.arange(4, dtype=jnp.int32)[None, :] * HB + (block_ids[:, None] + offset) % HB
    extra = jax.random.randint(jax.random.fold_in(key, 12), (BLOCKS, K - 5), 0, RB + 1)
    extra = jnp.where(extra == RB, RB + 4 * HB, extra)
    return jnp.concatenate([block_ids[:, None], sides, extra], axis=1).astype(jnp.int32)


def draw_send_lists(key, part):
    return jax.random.randint(jax.random.fold_in(key, 21), (N_LAT * N_LON, 4, HB), 0, RB).astype(jnp.int32)


def draw_region_map(key, part):
    rows_all = N_LAT * N_LON * RB * BLOCK
    tile = jnp.arange(rows_all, dtype=jnp.int32) // (RB * BLOCK)
    lat_pos = tile // N_LON
    lon_pos = tile % N_LON
    select = jax.random.randint(jax.random.fold_in(key, 31), (rows_all,), 0, 10)
    step_lon = jnp.where(select == 0, -1, jnp.where(select == 1, 1, 0))
    owner = lat_pos * N_LON + (lon_pos + step_lon + N_LON) % N_LON
    offset = jax.random.randint(jax.random.fold_in(key, 32), (rows_all,), 0, REG_DEV)
    return (owner * REG_DEV + offset).astype(jnp.int32)


def shard_levels(stream_key, shape, split, smallest, largest):
    level = 1.0
    for axis_at, shards_of in split:
        draws = jax.random.uniform(jax.random.fold_in(jax.random.fold_in(stream_key, 6), axis_at), (shards_of,), jnp.float32, smallest / len(split), largest / len(split))
        level = level * jnp.repeat(jnp.exp(draws), shape[axis_at] // shards_of).reshape((-1,) + (1,) * (len(shape) - 1 - axis_at))
    return level


def scatter_about(stream_key, extent, spread, most, shards=(), kind=jnp.bfloat16):
    factor_of = shard_levels(stream_key, extent, shards, -0.22, 0.18) if shards else 1.0
    entries = jax.random.normal(stream_key, extent, jnp.float32) * spread * factor_of
    return jnp.minimum(jnp.maximum(entries, -most), most).astype(kind)


def setup_inputs(seed: int = 0) -> dict:
    keys = jax.random.split(jax.random.key(seed), 11)
    state_init = scatter_about(keys[0], (NT, ROWS), 1.0, 6.0, ((1, 32),), jnp.float32)
    tangent_init = scatter_about(keys[1], (NT, ROWS), 1.0, 6.0, ((1, 32),), jnp.float32)
    coef_blocks = scatter_about(keys[2], (BLOCKS, K, BLOCK, BLOCK), (BLOCK * K) ** -0.5, 0.21875, ((0, 32),))
    column_lists = draw_column_lists(jax.random.fold_in(keys[10], 71), 0)
    send_lists = draw_send_lists(jax.random.fold_in(keys[10], 71), 0)
    implicit_blocks = scatter_about(keys[5], (BLOCKS, BLOCK, BLOCK), BLOCK ** -0.5, 0.5, ((0, 32),))
    uptake_rate = jnp.clip(jnp.exp(math.log(4.0) - 2.0794415 * jax.random.uniform(keys[6], (ROWS,), jnp.float32) ** shard_levels(keys[6], (ROWS,), ((0, 32),), -0.2, 0.2)), 0.5, 4.0)
    coupling = scatter_about(keys[7], (NT, NT), NT ** -0.5, 1.5, (), jnp.float32)
    region_map = draw_region_map(jax.random.fold_in(keys[10], 71), 0)
    coarse_inverse = scatter_about(keys[9], (NC, NC), (RB * BLOCK * N_LAT * N_LON) ** -0.5, 0.0234375, ((0, 32),), jnp.float32)
    return {"state_init": state_init, "tangent_init": tangent_init, "coef_blocks": coef_blocks, "column_lists": column_lists, "send_lists": send_lists, "implicit_blocks": implicit_blocks, "uptake_rate": uptake_rate, "coupling": coupling, "region_map": region_map, "coarse_inverse": coarse_inverse}


step_length = 0.5


def readable_blocks(rounded, send_lists):
    channels = rounded.shape[0]
    tiles = rounded.reshape(channels, N_LAT, N_LON, RB, BLOCK)
    sends = send_lists.reshape(N_LAT, N_LON, 4 * HB)
    lat_ids = jnp.arange(N_LAT)[:, None, None]
    lon_ids = jnp.arange(N_LON)[None, :, None]
    picked = tiles[:, lat_ids, lon_ids, sends].reshape(channels, N_LAT, N_LON, 4, HB, BLOCK)
    zero_row = jnp.zeros_like(picked[:, :1, :, 0])
    from_below = jnp.concatenate([zero_row, picked[:, :-1, :, 0]], axis=1)
    from_above = jnp.concatenate([picked[:, 1:, :, 1], zero_row], axis=1)
    from_west = jnp.roll(picked[:, :, :, 2], 1, axis=2)
    from_east = jnp.roll(picked[:, :, :, 3], -1, axis=2)
    empty = jnp.zeros((channels, N_LAT, N_LON, 1, BLOCK), rounded.dtype)
    return jnp.concatenate([tiles, from_below, from_above, from_west, from_east, empty], axis=3)


def transport(readable, column_lists, coef_blocks):
    lists = column_lists.reshape(N_LAT, N_LON, RB, K)
    coefs = coef_blocks.reshape(N_LAT, N_LON, RB, K, BLOCK, BLOCK)
    lon_ids = jnp.arange(N_LON)[:, None, None]

    def one_lat(items):
        ext_lat, list_lat, coef_lat = items
        gathered = ext_lat[:, lon_ids, list_lat]
        return jnp.einsum("cobkp,obkpq->cobq", gathered.astype(jnp.float32), coef_lat.astype(jnp.float32), precision=lax.Precision.HIGHEST)

    moved = lax.map(one_lat, (jnp.moveaxis(readable, 1, 0), lists, coefs))
    moved = jnp.moveaxis(moved, 0, 1)
    return moved.reshape(readable.shape[0], ROWS)


def reference(state_init, tangent_init, coef_blocks, column_lists, send_lists, implicit_blocks, uptake_rate, coupling, region_map, coarse_inverse):
    state = state_init
    tangent = tangent_init
    channels = 2 * NT
    for sweep_index in range(STEPS):
        stacked = jnp.concatenate([state, tangent], axis=0)
        rounded = stacked.astype(jnp.bfloat16)
        readable = readable_blocks(rounded, send_lists)
        moved = transport(readable, column_lists, coef_blocks)
        squared = state * state
        denom = 1.0 + squared
        uptake = uptake_rate * state / denom
        slope = uptake_rate * (1.0 - squared) / (denom * denom) * tangent
        sources = jnp.dot(coupling, jnp.concatenate([uptake, slope], axis=1), precision=lax.Precision.HIGHEST, preferred_element_type=jnp.float32)
        sources = jnp.concatenate([sources[:, :ROWS], sources[:, ROWS:]], axis=0)
        explicit = (stacked + moved + step_length * sources).astype(jnp.bfloat16)
        shaped = explicit.reshape(channels, BLOCKS, BLOCK).astype(jnp.float32)
        implicit = jnp.einsum("cbp,bpq->cbq", shaped, implicit_blocks.astype(jnp.float32), precision=lax.Precision.HIGHEST)
        implicit = implicit.reshape(channels, ROWS)
        state = implicit[:NT]
        tangent = implicit[NT:]
    residual = tangent - tangent_init
    totals = jax.ops.segment_sum(residual.T, region_map, num_segments=NC).T
    values = jnp.dot(totals, coarse_inverse.T, precision=lax.Precision.HIGHEST, preferred_element_type=jnp.float32)
    preconditioned = residual + jnp.take(values, region_map, axis=1)
    return state, preconditioned
```

```python
import functools

import jax
import jax.numpy as jnp
from jax import lax
from jax.experimental import pallas as pl
from jax.experimental.pallas import tpu as pltpu
from jax.sharding import PartitionSpec as P

BOTH = ("lat", "lon")
F32 = jnp.float32
BF16 = jnp.bfloat16
step_length = 0.5


def split2(value):
    high = value.astype(BF16)
    low = (value - high.astype(F32)).astype(BF16)
    return high, low


def vmem(count):
    return [pl.BlockSpec(memory_space=pltpu.VMEM)] * count


def smem(count):
    return [pl.BlockSpec(memory_space=pltpu.SMEM)] * count


def params():
    return pltpu.CompilerParams(vmem_limit_bytes=24 * 1024 * 1024)


def pick_sends(sends_ref, meta_ref, rounded_of, outs, halo):
    lat_odd = meta_ref[0] % 2
    lon_odd = meta_ref[1] % 2
    lists = (lat_odd, 1 - lat_odd, 2 + lon_odd, 3 - lon_odd)
    for out_ref, which in zip(outs, lists):
        for at in range(halo):
            piece = rounded_of(sends_ref[which, at])
            out_ref[at * piece.shape[0] : (at + 1) * piece.shape[0], :] = piece


def first_kernel(sends_ref, meta_ref, state_ref, tangent_ref, inverse_ref, *outs, halo, block):
    def rounded_of(index):
        lanes = pl.ds(pl.multiple_of(index * block, block), block)
        return jnp.concatenate([state_ref[:, lanes], tangent_ref[:, lanes]], axis=0).astype(BF16)

    pick_sends(sends_ref, meta_ref, rounded_of, outs, halo)
    channels = 2 * state_ref.shape[0]
    regions, width = inverse_ref.shape
    for at in range(width // block):
        high, low = split2(inverse_ref[:, at * block : (at + 1) * block])
        piece = jnp.concatenate([high.astype(F32), low.astype(F32)], axis=0).astype(BF16)
        start = halo * channels + at * 2 * regions
        for out_ref in outs[2:]:
            out_ref[start : start + 2 * regions, :] = piece


def own_kernel(cols_ref, state_ref, tangent_ref, coef_ref, rate_ref, coupling_ref, acc_ref, own_ref, *, block):
    tracers = state_ref.shape[0]
    blocks, entries = coef_ref.shape[:2]
    own_ref[blocks] = jnp.zeros(own_ref.shape[1:], BF16)
    high, low = split2(coupling_ref[...] * step_length)
    zero = jnp.zeros_like(high)
    mix_high = jnp.concatenate(
        [jnp.concatenate([high, zero], axis=1), jnp.concatenate([zero, high], axis=1)], axis=0
    )
    mix_low = jnp.concatenate(
        [jnp.concatenate([low, zero], axis=1), jnp.concatenate([zero, low], axis=1)], axis=0
    )
    mix = jnp.concatenate([mix_high, mix_high, mix_low], axis=1)
    for b in range(blocks):
        lanes = slice(b * block, (b + 1) * block)
        stacked = jnp.concatenate([state_ref[:, lanes], tangent_ref[:, lanes]], axis=0)
        own_ref[b] = stacked.astype(BF16)
    for b in range(blocks):
        lanes = slice(b * block, (b + 1) * block)
        state = state_ref[:, lanes]
        tangent = tangent_ref[:, lanes]
        rate = rate_ref[:, lanes]
        squared = state * state
        inverse = 1.0 / (1.0 + squared)
        scaled = rate * inverse
        uptake = scaled * state
        slope = scaled * inverse * (1.0 - squared) * tangent
        term_high, term_low = split2(jnp.concatenate([uptake, slope], axis=0))
        terms = jnp.concatenate([term_high, term_low, term_high], axis=0)
        total = jnp.concatenate([state, tangent], axis=0)
        total += jnp.dot(mix, terms, preferred_element_type=F32)
        total += jnp.dot(own_ref[b], coef_ref[b, 0], preferred_element_type=F32)
        for k in range(5, entries):
            index = jnp.minimum(cols_ref[b, k], blocks)
            total += jnp.dot(own_ref[index], coef_ref[b, k], preferred_element_type=F32)
        acc_ref[:, lanes] = total


def halo_blocks(meta_ref, recvs, halo_ref, halo):
    channels = halo_ref.shape[1]
    for at, recv in enumerate(recvs):
        for s in range(halo):
            piece = recv[s * channels : (s + 1) * channels, :]
            if at == 1:
                piece = jnp.where(meta_ref[2] > 0, jnp.zeros_like(piece), piece)
            halo_ref[at * halo + s] = piece


def solved(b, cols_ref, meta_ref, acc_ref, coef_ref, implicit_ref, halo_ref, halo, block):
    blocks = coef_ref.shape[0]
    lat_odd = meta_ref[0] % 2
    lon_odd = meta_ref[1] % 2
    shifts = (1 - lat_odd, lat_odd, 3 - lon_odd, 2 + lon_odd)
    pieces = []
    for d in range(4):
        slot = shifts[d] * halo + cols_ref[b, 1 + d] - (blocks + d * halo)
        pieces.append(halo_ref[slot])
    gathered = jnp.concatenate(pieces, axis=1)
    weights = coef_ref[b, 1:5].reshape(4 * block, block)
    moved = jnp.dot(gathered, weights, preferred_element_type=F32)
    explicit = (acc_ref[:, b * block : (b + 1) * block] + moved).astype(BF16)
    return jnp.dot(explicit, implicit_ref[b], preferred_element_type=F32)


def step_kernel(
    cols_ref, meta_ref, sends_ref, acc_ref, a_ref, b_ref, c_ref, r_ref, coef_ref, implicit_ref,
    state_ref, tangent_ref, a_out, b_out, c_out, r_out, halo_ref, own_ref, *, halo, block,
):
    halo_blocks(meta_ref, (a_ref, b_ref, c_ref, r_ref), halo_ref, halo)
    tracers = state_ref.shape[0]
    for b in range(coef_ref.shape[0]):
        lanes = slice(b * block, (b + 1) * block)
        new = solved(b, cols_ref, meta_ref, acc_ref, coef_ref, implicit_ref, halo_ref, halo, block)
        state_ref[:, lanes] = new[:tracers]
        tangent_ref[:, lanes] = new[tracers:]
        own_ref[b] = new.astype(BF16)
    pick_sends(sends_ref, meta_ref, lambda index: own_ref[index], (a_out, b_out, c_out, r_out), halo)


def last_kernel(
    cols_ref, meta_ref, acc_ref, a_ref, b_ref, c_ref, r_ref, coef_ref, implicit_ref, start_ref, region_ref,
    state_ref, residual_ref, totals_ref, halo_ref, *, halo, block, row_regions,
):
    halo_blocks(meta_ref, (a_ref, b_ref, c_ref, r_ref), halo_ref, halo)
    tracers = state_ref.shape[0]
    first = meta_ref[0] * row_regions
    sums = jnp.zeros((2 * tracers, row_regions), F32)
    for b in range(coef_ref.shape[0]):
        lanes = slice(b * block, (b + 1) * block)
        new = solved(b, cols_ref, meta_ref, acc_ref, coef_ref, implicit_ref, halo_ref, halo, block)
        state_ref[:, lanes] = new[:tracers]
        residual = new[tracers:] - start_ref[:, lanes]
        residual_ref[:, lanes] = residual
        both = jnp.concatenate(split2(residual), axis=0)
        ids = lax.broadcasted_iota(jnp.int32, (row_regions, block), 0) + first
        chosen = (ids == region_ref[:, lanes]).astype(F32).astype(BF16)
        sums += lax.dot_general(both, chosen, (((1,), (1,)), ((), ())), preferred_element_type=F32)
    sums = sums[:tracers] + sums[tracers:]
    width = totals_ref.shape[1]
    if width > row_regions:
        sums = jnp.concatenate([sums, jnp.zeros((tracers, width - row_regions), F32)], axis=1)
    totals_ref[...] = pltpu.roll(sums, first, 1)


def correct_kernel(
    meta_ref, totals_ref, inverse_ref, c_ref, r_ref, region_ref, residual_ref, out_ref, *, skip, block
):
    regions, width = inverse_ref.shape
    tracers = totals_ref.shape[0]
    t_high, t_low = split2(totals_ref[...])
    both = jnp.concatenate([t_high, t_low], axis=0)
    values = jnp.zeros((tracers, 3 * regions), F32)
    nt = (((1,), (1,)), ((), ()))
    for at in range(width // block):
        lanes = slice(at * block, (at + 1) * block)
        rows = slice(skip + at * 2 * regions, skip + (at + 1) * 2 * regions)
        own_high, own_low = split2(inverse_ref[:, lanes])
        c_all = c_ref[rows, :].astype(F32)
        r_all = r_ref[rows, :].astype(F32)
        high = jnp.concatenate([own_high.astype(F32), c_all[:regions], r_all[:regions]], axis=0).astype(BF16)
        low = jnp.concatenate([own_low.astype(F32), c_all[regions:], r_all[regions:]], axis=0).astype(BF16)
        part = lax.dot_general(both[:, lanes], high, nt, preferred_element_type=F32)
        values += part[:tracers] + part[tracers:]
        values += lax.dot_general(t_high[:, lanes], low, nt, preferred_element_type=F32)
    v_high, v_low = split2(values)
    rows_id = lax.broadcasted_iota(jnp.int32, (3 * regions, 1), 0)
    group = rows_id // regions
    base = jnp.where(group == 0, meta_ref[3], jnp.where(group == 1, meta_ref[4], meta_ref[5]))
    ids = base * regions + rows_id % regions
    chosen = (ids == region_ref[...]).astype(F32).astype(BF16)
    out = jnp.dot(v_high, chosen, preferred_element_type=F32)
    out += jnp.dot(v_low, chosen, preferred_element_type=F32)
    out_ref[...] = residual_ref[...] + out


def partners(n_lat, n_lon):
    def flat(la, lo):
        return la * n_lon + lo

    lat_even, lat_odd, core, ring = [], [], [], []
    for la in range(n_lat):
        for lo in range(n_lon):
            me = flat(la, lo)
            lat_even.append((me, flat(la ^ 1, lo)))
            if la in (0, n_lat - 1):
                lat_odd.append((me, flat(la, lo ^ 1)))
            else:
                lat_odd.append((me, flat(la + 1 if la % 2 else la - 1, lo)))
            core.append((me, flat(la, lo ^ 1)))
            ring.append((me, flat(la, (lo + 1 if lo % 2 else lo - 1) % n_lon)))
    return lat_even, lat_odd, core, ring


def local(
    state_init, tangent_init, coef_blocks, column_lists, send_lists, implicit_blocks,
    uptake_rate, coupling, region_map, coarse_inverse,
):
    n_lat, n_lon = lax.axis_size("lat"), lax.axis_size("lon")
    tracers, rows = state_init.shape
    blocks, entries, block = coef_blocks.shape[:3]
    halo = send_lists.shape[2]
    channels = 2 * tracers
    regions, width = coarse_inverse.shape
    devices = n_lat * n_lon
    lat_pos, lon_pos = lax.axis_index("lat"), lax.axis_index("lon")
    edge = ((lat_pos == 0) | (lat_pos == n_lat - 1)).astype(jnp.int32)
    ring_lon = (lon_pos + jnp.where(lon_pos % 2 == 0, n_lon - 1, 1)) % n_lon
    base = lat_pos * n_lon
    meta = jnp.stack([lat_pos, lon_pos, edge, base + lon_pos, base + (lon_pos ^ 1), base + ring_lon])
    meta = meta.astype(jnp.int32)
    sends = send_lists[0]
    rate = uptake_rate.reshape(1, rows)
    region = region_map.reshape(1, rows)
    perms = partners(n_lat, n_lon)

    halo_shape = jax.ShapeDtypeStruct((halo * channels, block), BF16)
    lon_shape = jax.ShapeDtypeStruct((halo * channels + 2 * regions * (width // block), block), BF16)
    field = jax.ShapeDtypeStruct((tracers, rows), F32)

    first = pl.pallas_call(
        functools.partial(first_kernel, halo=halo, block=block),
        out_shape=(halo_shape, halo_shape, lon_shape, lon_shape),
        in_specs=smem(2) + vmem(3),
        out_specs=tuple(vmem(4)),
        compiler_params=params(),
        name="first",
    )
    own = pl.pallas_call(
        functools.partial(own_kernel, block=block),
        out_shape=jax.ShapeDtypeStruct((channels, rows), F32),
        in_specs=smem(1) + vmem(5),
        out_specs=vmem(1)[0],
        scratch_shapes=[pltpu.VMEM((blocks + 1, channels, block), BF16)],
        compiler_params=params(),
        cost_estimate=pl.CostEstimate(flops=2 * 10**9, bytes_accessed=4 * 10**6, transcendentals=0),
        name="own",
    )
    step = pl.pallas_call(
        functools.partial(step_kernel, halo=halo, block=block),
        out_shape=(field, field) + (halo_shape,) * 4,
        in_specs=smem(3) + vmem(7),
        out_specs=tuple(vmem(6)),
        scratch_shapes=[
            pltpu.VMEM((4 * halo, channels, block), BF16),
            pltpu.VMEM((blocks, channels, block), BF16),
        ],
        compiler_params=params(),
        name="step",
    )
    last = pl.pallas_call(
        functools.partial(last_kernel, halo=halo, block=block, row_regions=n_lon * regions),
        out_shape=(field, field, jax.ShapeDtypeStruct((tracers, width), F32)),
        in_specs=smem(2) + vmem(9),
        out_specs=tuple(vmem(3)),
        scratch_shapes=[pltpu.VMEM((4 * halo, channels, block), BF16)],
        compiler_params=params(),
        name="last",
    )
    correct = pl.pallas_call(
        functools.partial(correct_kernel, skip=halo * channels, block=block),
        out_shape=field,
        in_specs=smem(1) + vmem(6),
        out_specs=vmem(1)[0],
        compiler_params=params(),
        name="correct",
    )

    def exchange(sent):
        return [lax.ppermute(value, BOTH, pairs) for value, pairs in zip(sent, perms)]

    sent = first(sends, meta, state_init, tangent_init, coarse_inverse)
    got1 = exchange(sent)
    acc = own(column_lists, state_init, tangent_init, coef_blocks, rate, coupling)
    state, tangent, *sent = step(column_lists, meta, sends, acc, *got1, coef_blocks, implicit_blocks)
    got2 = exchange(sent)
    acc = own(column_lists, state, tangent, coef_blocks, rate, coupling)
    final_state, residual, totals = last(
        column_lists, meta, acc, *got2, coef_blocks, implicit_blocks, tangent_init, region
    )
    bit = 1
    while bit < devices:
        mask = bit | 1
        totals = totals + lax.ppermute(totals, BOTH, [(i, i ^ mask) for i in range(devices)])
        bit *= 2
    preconditioned = correct(meta, totals, coarse_inverse, got1[2], got1[3], region, residual)
    return final_state, preconditioned


def solution(mesh):
    placed = (
        P(None, BOTH),
        P(None, BOTH),
        P(BOTH, None, None, None),
        P(BOTH, None),
        P(BOTH, None, None),
        P(BOTH, None, None),
        P(BOTH),
        P(),
        P(BOTH),
        P(BOTH, None),
    )
    return jax.shard_map(
        local,
        mesh=mesh,
        in_specs=placed,
        out_specs=(P(None, BOTH), P(None, BOTH)),
        check_vma=False,
    )
```

```python
import functools

import jax
import jax.numpy as jnp
from jax import lax
from jax.experimental import pallas as pl
from jax.experimental.pallas import tpu as pltpu
from jax.sharding import PartitionSpec as P

BOTH = ("lat", "lon")
F32 = jnp.float32
BF16 = jnp.bfloat16
step_length = 0.5


def split2(value):
    high = value.astype(BF16)
    low = (value - high.astype(F32)).astype(BF16)
    return high, low


def vmem(count):
    return [pl.BlockSpec(memory_space=pltpu.VMEM)] * count


def smem(count):
    return [pl.BlockSpec(memory_space=pltpu.SMEM)] * count


def params():
    return pltpu.CompilerParams(vmem_limit_bytes=24 * 1024 * 1024)


def pick_sends(sends_ref, meta_ref, rounded_of, outs, halo):
    lat_odd = meta_ref[0] % 2
    lon_odd = meta_ref[1] % 2
    lists = (lat_odd, 1 - lat_odd, 2 + lon_odd, 3 - lon_odd)
    for out_ref, which in zip(outs, lists):
        for at in range(halo):
            piece = rounded_of(sends_ref[at, which])
            out_ref[at * piece.shape[0] : (at + 1) * piece.shape[0], :] = piece


def start_copies(sources, targets, sems, base=0):
    copies = []
    for at, (source, target) in enumerate(zip(sources, targets)):
        copy = pltpu.make_async_copy(source, target, sems.at[base + at])
        copy.start()
        copies.append(copy)
    return copies


def first_kernel(
    meta_ref, sends_hbm, state_hbm, tangent_hbm, inverse_hbm, cols_hbm, rate_hbm, coupling_hbm, region_hbm,
    a_out, b_out, c_out, r_out, state_ref, tangent_ref, inverse_ref, cols_ref, rate_ref, coupling_ref, region_ref,
    sends_out, sends_ref, sems, *, halo, block,
):
    copies = start_copies(
        (sends_hbm, state_hbm, tangent_hbm, inverse_hbm, cols_hbm, rate_hbm, coupling_hbm, region_hbm, sends_hbm),
        (sends_ref, state_ref, tangent_ref, inverse_ref, cols_ref, rate_ref, coupling_ref, region_ref, sends_out),
        sems,
    )
    for copy in copies[:4]:
        copy.wait()

    def rounded_of(index):
        lanes = pl.ds(pl.multiple_of(index * block, block), block)
        return jnp.concatenate([state_ref[:, lanes], tangent_ref[:, lanes]], axis=0).astype(BF16)

    pick_sends(sends_ref, meta_ref, rounded_of, (a_out, b_out, c_out, r_out), halo)
    channels = 2 * state_ref.shape[0]
    regions, width = inverse_ref.shape
    for at in range(width // block):
        high, low = split2(inverse_ref[:, at * block : (at + 1) * block])
        piece = jnp.concatenate([high.astype(F32), low.astype(F32)], axis=0).astype(BF16)
        start = halo * channels + at * 2 * regions
        for out_ref in (c_out, r_out):
            out_ref[start : start + 2 * regions, :] = piece
    for copy in copies[4:]:
        copy.wait()


def own_terms(cols_ref, state_ref, tangent_ref, coef_ref, rate_ref, coupling_ref, acc_ref, own_ref, block, ready):
    tracers = state_ref.shape[0]
    blocks, entries = coef_ref.shape[:2]
    own_ref[blocks] = jnp.zeros(own_ref.shape[1:], BF16)
    high, low = split2(coupling_ref[...] * step_length)
    zero = jnp.zeros_like(high)
    mix_high = jnp.concatenate(
        [jnp.concatenate([high, zero], axis=1), jnp.concatenate([zero, high], axis=1)], axis=0
    )
    mix_low = jnp.concatenate(
        [jnp.concatenate([low, zero], axis=1), jnp.concatenate([zero, low], axis=1)], axis=0
    )
    mix = jnp.concatenate([mix_high, mix_high, mix_low], axis=1)
    for b in range(blocks):
        lanes = slice(b * block, (b + 1) * block)
        state = state_ref[:, lanes]
        tangent = tangent_ref[:, lanes]
        rate = rate_ref[:, lanes]
        squared = state * state
        inverse = 1.0 / (1.0 + squared)
        scaled = rate * inverse
        uptake = scaled * state
        slope = scaled * inverse * (1.0 - squared) * tangent
        term_high, term_low = split2(jnp.concatenate([uptake, slope], axis=0))
        terms = jnp.concatenate([term_high, term_low, term_high], axis=0)
        stacked = jnp.concatenate([state, tangent], axis=0)
        own_ref[b] = stacked.astype(BF16)
        acc_ref[:, lanes] = stacked + jnp.dot(mix, terms, preferred_element_type=F32)
    for b in range(blocks):
        lanes = slice(b * block, (b + 1) * block)
        ready(b)
        total = acc_ref[:, lanes] + jnp.dot(own_ref[b], coef_ref[b, 0], preferred_element_type=F32)
        for k in range(5, entries):
            index = jnp.minimum(cols_ref[k, b], blocks)
            total += jnp.dot(own_ref[index], coef_ref[b, k], preferred_element_type=F32)
        acc_ref[:, lanes] = total


def own_kernel(cols_ref, state_ref, tangent_ref, coef_ref, rate_ref, coupling_ref, acc_ref, own_ref, *, block):
    own_terms(
        cols_ref, state_ref, tangent_ref, coef_ref, rate_ref, coupling_ref, acc_ref, own_ref, block, lambda b: None
    )


def load_kernel(
    cols_ref, state_ref, tangent_ref, rate_ref, coupling_ref, coef_hbm, implicit_hbm,
    acc_ref, coef_ref, implicit_ref, own_ref, sems, *, block,
):
    blocks = coef_ref.shape[0]
    copies = start_copies(
        [coef_hbm.at[b] for b in range(blocks)], [coef_ref.at[b] for b in range(blocks)], sems
    )
    copies += start_copies((implicit_hbm,), (implicit_ref,), sems, blocks)
    own_terms(
        cols_ref, state_ref, tangent_ref, coef_ref, rate_ref, coupling_ref, acc_ref, own_ref, block,
        lambda b: copies[b].wait(),
    )
    copies[blocks].wait()


def halo_blocks(meta_ref, recvs, halo_ref, halo):
    channels = halo_ref.shape[1]
    for at, recv in enumerate(recvs):
        for s in range(halo):
            piece = recv[s * channels : (s + 1) * channels, :]
            if at == 1:
                piece = jnp.where(meta_ref[2] > 0, jnp.zeros_like(piece), piece)
            halo_ref[at * halo + s] = piece


def transported(cols_ref, meta_ref, acc_ref, coef_ref, halo_ref, explicit_ref, halo, block):
    blocks = coef_ref.shape[0]
    lat_odd = meta_ref[0] % 2
    lon_odd = meta_ref[1] % 2
    shifts = (1 - lat_odd, lat_odd, 3 - lon_odd, 2 + lon_odd)
    offsets = [shifts[d] * halo - (blocks + d * halo) for d in range(4)]
    for b in range(blocks):
        pieces = [halo_ref[offsets[d] + cols_ref[1 + d, b]] for d in range(4)]
        gathered = jnp.concatenate(pieces, axis=1)
        weights = coef_ref[b, 1:5].reshape(4 * block, block)
        moved = jnp.dot(gathered, weights, preferred_element_type=F32)
        explicit_ref[b] = (acc_ref[:, b * block : (b + 1) * block] + moved).astype(BF16)


def step_kernel(
    cols_ref, meta_ref, sends_ref, acc_ref, a_ref, b_ref, c_ref, r_ref, coef_ref, implicit_ref,
    state_ref, tangent_ref, a_out, b_out, c_out, r_out, halo_ref, explicit_ref, own_ref, *, halo, block,
):
    halo_blocks(meta_ref, (a_ref, b_ref, c_ref, r_ref), halo_ref, halo)
    tracers = state_ref.shape[0]
    transported(cols_ref, meta_ref, acc_ref, coef_ref, halo_ref, explicit_ref, halo, block)
    for b in range(coef_ref.shape[0]):
        lanes = slice(b * block, (b + 1) * block)
        new = jnp.dot(explicit_ref[b], implicit_ref[b], preferred_element_type=F32)
        state_ref[:, lanes] = new[:tracers]
        tangent_ref[:, lanes] = new[tracers:]
        own_ref[b] = new.astype(BF16)
    pick_sends(sends_ref, meta_ref, lambda index: own_ref[index], (a_out, b_out, c_out, r_out), halo)


def last_kernel(
    cols_ref, meta_ref, acc_ref, a_ref, b_ref, c_ref, r_ref, coef_ref, implicit_ref, start_ref, region_ref,
    state_ref, residual_ref, totals_ref, halo_ref, explicit_ref, both_ref, *, halo, block, row_regions,
):
    halo_blocks(meta_ref, (a_ref, b_ref, c_ref, r_ref), halo_ref, halo)
    tracers, rows = state_ref.shape
    first = meta_ref[0] * row_regions
    transported(cols_ref, meta_ref, acc_ref, coef_ref, halo_ref, explicit_ref, halo, block)
    for b in range(coef_ref.shape[0]):
        lanes = slice(b * block, (b + 1) * block)
        new = jnp.dot(explicit_ref[b], implicit_ref[b], preferred_element_type=F32)
        state_ref[:, lanes] = new[:tracers]
        residual = new[tracers:] - start_ref[:, lanes]
        residual_ref[:, lanes] = residual
        high, low = split2(residual)
        both_ref[:tracers, lanes] = high
        both_ref[tracers:, lanes] = low
    ids = lax.broadcasted_iota(jnp.int32, (row_regions, rows), 0) + first
    chosen = (ids == region_ref[...]).astype(F32).astype(BF16)
    sums = lax.dot_general(both_ref[...], chosen, (((1,), (1,)), ((), ())), preferred_element_type=F32)
    sums = sums[:tracers] + sums[tracers:]
    width = totals_ref.shape[1]
    if width > row_regions:
        sums = jnp.concatenate([sums, jnp.zeros((tracers, width - row_regions), F32)], axis=1)
    totals_ref[...] = pltpu.roll(sums, first, 1)


def correct_kernel(
    meta_ref, totals_ref, inverse_ref, c_ref, r_ref, region_ref, residual_ref, out_ref, *, skip, block
):
    regions, width = inverse_ref.shape
    tracers = totals_ref.shape[0]
    t_high, t_low = split2(totals_ref[...])
    both = jnp.concatenate([t_high, t_low], axis=0)
    values = jnp.zeros((tracers, 3 * regions), F32)
    nt = (((1,), (1,)), ((), ()))
    for at in range(width // block):
        lanes = slice(at * block, (at + 1) * block)
        rows = slice(skip + at * 2 * regions, skip + (at + 1) * 2 * regions)
        own_high, own_low = split2(inverse_ref[:, lanes])
        c_all = c_ref[rows, :].astype(F32)
        r_all = r_ref[rows, :].astype(F32)
        high = jnp.concatenate([own_high.astype(F32), c_all[:regions], r_all[:regions]], axis=0).astype(BF16)
        low = jnp.concatenate([own_low.astype(F32), c_all[regions:], r_all[regions:]], axis=0).astype(BF16)
        part = lax.dot_general(both[:, lanes], high, nt, preferred_element_type=F32)
        values += part[:tracers] + part[tracers:]
        values += lax.dot_general(t_high[:, lanes], low, nt, preferred_element_type=F32)
    v_high, v_low = split2(values)
    rows_id = lax.broadcasted_iota(jnp.int32, (3 * regions, 1), 0)
    group = rows_id // regions
    base = jnp.where(group == 0, meta_ref[3], jnp.where(group == 1, meta_ref[4], meta_ref[5]))
    ids = base * regions + rows_id % regions
    chosen = (ids == region_ref[...]).astype(F32).astype(BF16)
    out = jnp.dot(v_high, chosen, preferred_element_type=F32)
    out += jnp.dot(v_low, chosen, preferred_element_type=F32)
    out_ref[...] = residual_ref[...] + out


def partners(n_lat, n_lon):
    def flat(la, lo):
        return la * n_lon + lo

    lat_even, lat_odd, core, ring = [], [], [], []
    for la in range(n_lat):
        for lo in range(n_lon):
            me = flat(la, lo)
            lat_even.append((me, flat(la ^ 1, lo)))
            if la in (0, n_lat - 1):
                lat_odd.append((me, flat(la, lo ^ 1)))
            else:
                lat_odd.append((me, flat(la + 1 if la % 2 else la - 1, lo)))
            core.append((me, flat(la, lo ^ 1)))
            ring.append((me, flat(la, (lo + 1 if lo % 2 else lo - 1) % n_lon)))
    return lat_even, lat_odd, core, ring


def local(
    state_init, tangent_init, coef_blocks, column_lists, send_lists, implicit_blocks,
    uptake_rate, coupling, region_map, coarse_inverse,
):
    n_lat, n_lon = lax.axis_size("lat"), lax.axis_size("lon")
    tracers, rows = state_init.shape
    blocks, entries, block = coef_blocks.shape[:3]
    halo = send_lists.shape[2]
    channels = 2 * tracers
    regions, width = coarse_inverse.shape
    devices = n_lat * n_lon
    lat_pos, lon_pos = lax.axis_index("lat"), lax.axis_index("lon")
    edge = ((lat_pos == 0) | (lat_pos == n_lat - 1)).astype(jnp.int32)
    ring_lon = (lon_pos + jnp.where(lon_pos % 2 == 0, n_lon - 1, 1)) % n_lon
    base = lat_pos * n_lon
    meta = jnp.stack([lat_pos, lon_pos, edge, base + lon_pos, base + (lon_pos ^ 1), base + ring_lon])
    meta = meta.astype(jnp.int32)
    sends = send_lists[0].T
    cols = column_lists.T
    rate = uptake_rate.reshape(1, rows)
    region = region_map.reshape(1, rows)
    perms = partners(n_lat, n_lon)

    halo_shape = jax.ShapeDtypeStruct((halo * channels, block), BF16)
    lon_shape = jax.ShapeDtypeStruct((halo * channels + 2 * regions * (width // block), block), BF16)
    field = jax.ShapeDtypeStruct((tracers, rows), F32)
    acc_shape = jax.ShapeDtypeStruct((channels, rows), F32)
    like = lambda value: jax.ShapeDtypeStruct(value.shape, value.dtype)
    halo_scratch = pltpu.VMEM((4 * halo, channels, block), BF16)
    block_scratch = pltpu.VMEM((blocks, channels, block), BF16)
    own_scratch = pltpu.VMEM((blocks + 1, channels, block), BF16)
    dma = pltpu.SemaphoreType.DMA

    def call(kernel, name, outs, n_smem, n_vmem, n_any, scratch, flops=0, **static):
        return pl.pallas_call(
            functools.partial(kernel, block=block, **static),
            out_shape=outs,
            in_specs=smem(n_smem) + vmem(n_vmem) + [pl.BlockSpec(memory_space=pltpu.HBM)] * n_any,
            out_specs=jax.tree.map(lambda _: vmem(1)[0], outs),
            scratch_shapes=scratch,
            compiler_params=params(),
            cost_estimate=pl.CostEstimate(flops=flops, bytes_accessed=10**6, transcendentals=0),
            name=name,
        )

    smalls = (state_init, tangent_init, coarse_inverse, cols, rate, coupling, region)
    first = call(
        first_kernel, "first",
        (halo_shape, halo_shape, lon_shape, lon_shape) + tuple(like(v) for v in smalls) + (like(sends),),
        1, 0, 8, [pltpu.SMEM(sends.shape, jnp.int32), dma((9,))], halo=halo,
    )
    load = call(
        load_kernel, "load", (acc_shape, like(coef_blocks), like(implicit_blocks)), 1, 4, 2,
        [own_scratch, dma((blocks + 1,))], flops=10**9,
    )
    own = call(own_kernel, "own", acc_shape, 1, 5, 0, [own_scratch], flops=10**9)
    step = call(
        step_kernel, "step", (field, field) + (halo_shape,) * 4, 3, 7, 0,
        [halo_scratch, block_scratch, block_scratch], halo=halo,
    )
    last = call(
        last_kernel, "last", (field, field, jax.ShapeDtypeStruct((tracers, width), F32)), 2, 9, 0,
        [halo_scratch, block_scratch, pltpu.VMEM((channels, rows), BF16)],
        halo=halo, row_regions=n_lon * regions,
    )
    correct = call(correct_kernel, "correct", field, 1, 6, 0, [], skip=halo * channels)

    def exchange(sent):
        return [lax.ppermute(value, BOTH, pairs) for value, pairs in zip(sent, perms)]

    far = lambda value: pltpu.with_memory_space_constraint(value, pltpu.HBM)
    *sent, state, start, inverse, cols, rate, coupling, region, sends = first(
        meta, *map(far, (sends, state_init, tangent_init, coarse_inverse, cols, rate, coupling, region))
    )
    got1 = exchange(sent)
    acc, coef, implicit = load(cols, state, start, rate, coupling, far(coef_blocks), far(implicit_blocks))
    state, tangent, *sent = step(cols, meta, sends, acc, *got1, coef, implicit)
    got2 = exchange(sent)
    acc = own(cols, state, tangent, coef, rate, coupling)
    final_state, residual, totals = last(cols, meta, acc, *got2, coef, implicit, start, region)
    bit = 1
    while bit < devices:
        mask = bit | 1
        totals = totals + lax.ppermute(totals, BOTH, [(i, i ^ mask) for i in range(devices)])
        bit *= 2
    preconditioned = correct(meta, totals, inverse, got1[2], got1[3], region, residual)
    return final_state, preconditioned


def solution(mesh):
    placed = (
        P(None, BOTH),
        P(None, BOTH),
        P(BOTH, None, None, None),
        P(BOTH, None),
        P(BOTH, None, None),
        P(BOTH, None, None),
        P(BOTH),
        P(),
        P(BOTH),
        P(BOTH, None),
    )
    return jax.shard_map(
        local,
        mesh=mesh,
        in_specs=placed,
        out_specs=(P(None, BOTH), P(None, BOTH)),
        check_vma=False,
    )
```

```python
import functools

import jax
import jax.numpy as jnp
from jax import lax
from jax.experimental import pallas as pl
from jax.experimental.pallas import tpu as pltpu
from jax.sharding import PartitionSpec as P

BOTH = ("lat", "lon")
F32 = jnp.float32
BF16 = jnp.bfloat16
step_length = 0.5


def split2(value):
    high = value.astype(BF16)
    low = (value - high.astype(F32)).astype(BF16)
    return high, low


def vmem(count):
    return [pl.BlockSpec(memory_space=pltpu.VMEM)] * count


def smem(count):
    return [pl.BlockSpec(memory_space=pltpu.SMEM)] * count


def params():
    return pltpu.CompilerParams(vmem_limit_bytes=24 * 1024 * 1024)


def pick_sends(sends_ref, meta_ref, rounded_of, outs, halo):
    lat_odd = meta_ref[0] % 2
    lon_odd = meta_ref[1] % 2
    lists = (lat_odd, 1 - lat_odd, 2 + lon_odd, 3 - lon_odd)
    for out_ref, which in zip(outs, lists):
        for at in range(halo):
            piece = rounded_of(sends_ref[at, which])
            out_ref[at * piece.shape[0] : (at + 1) * piece.shape[0], :] = piece


def start_copies(sources, targets, sems, base=0):
    copies = []
    for at, (source, target) in enumerate(zip(sources, targets)):
        copy = pltpu.make_async_copy(source, target, sems.at[base + at])
        copy.start()
        copies.append(copy)
    return copies


def first_kernel(
    meta_ref, sends_hbm, state_hbm, tangent_hbm, inverse_hbm, cols_hbm, rate_hbm, coupling_hbm, region_hbm,
    a_out, b_out, c_out, r_out, state_ref, tangent_ref, inverse_ref, cols_ref, rate_ref, coupling_ref, region_ref,
    sends_out, sends_ref, sems, *, halo, block,
):
    copies = start_copies(
        (sends_hbm, state_hbm, tangent_hbm, inverse_hbm, cols_hbm, rate_hbm, coupling_hbm, region_hbm, sends_hbm),
        (sends_ref, state_ref, tangent_ref, inverse_ref, cols_ref, rate_ref, coupling_ref, region_ref, sends_out),
        sems,
    )
    for copy in copies[:4]:
        copy.wait()

    def rounded_of(index):
        lanes = pl.ds(pl.multiple_of(index * block, block), block)
        return jnp.concatenate([state_ref[:, lanes], tangent_ref[:, lanes]], axis=0).astype(BF16)

    pick_sends(sends_ref, meta_ref, rounded_of, (a_out, b_out, c_out, r_out), halo)
    channels = 2 * state_ref.shape[0]
    regions, width = inverse_ref.shape
    for at in range(width // block):
        high, low = split2(inverse_ref[:, at * block : (at + 1) * block])
        piece = jnp.concatenate([high.astype(F32), low.astype(F32)], axis=0).astype(BF16)
        start = halo * channels + at * 2 * regions
        for out_ref in (c_out, r_out):
            out_ref[start : start + 2 * regions, :] = piece
    for copy in copies[4:]:
        copy.wait()


def own_terms(cols_ref, state_ref, tangent_ref, coef_ref, rate_ref, coupling_ref, acc_ref, own_ref, block, ready):
    tracers = state_ref.shape[0]
    blocks, entries = coef_ref.shape[:2]
    own_ref[blocks] = jnp.zeros(own_ref.shape[1:], BF16)
    high, low = split2(coupling_ref[...] * step_length)
    zero = jnp.zeros_like(high)
    mix_high = jnp.concatenate(
        [jnp.concatenate([high, zero], axis=1), jnp.concatenate([zero, high], axis=1)], axis=0
    )
    mix_low = jnp.concatenate(
        [jnp.concatenate([low, zero], axis=1), jnp.concatenate([zero, low], axis=1)], axis=0
    )
    mix = jnp.concatenate([mix_high, mix_high, mix_low], axis=1)
    for b in range(blocks):
        lanes = slice(b * block, (b + 1) * block)
        state = state_ref[:, lanes]
        tangent = tangent_ref[:, lanes]
        rate = rate_ref[:, lanes]
        squared = state * state
        inverse = 1.0 / (1.0 + squared)
        scaled = rate * inverse
        uptake = scaled * state
        slope = scaled * inverse * (1.0 - squared) * tangent
        term_high, term_low = split2(jnp.concatenate([uptake, slope], axis=0))
        terms = jnp.concatenate([term_high, term_low, term_high], axis=0)
        stacked = jnp.concatenate([state, tangent], axis=0)
        own_ref[b] = stacked.astype(BF16)
        acc_ref[:, lanes] = stacked + jnp.dot(mix, terms, preferred_element_type=F32)
    for b in range(blocks):
        lanes = slice(b * block, (b + 1) * block)
        ready(b)
        total = acc_ref[:, lanes] + jnp.dot(own_ref[b], coef_ref[b, 0], preferred_element_type=F32)
        for k in range(5, entries):
            index = jnp.minimum(cols_ref[k, b], blocks)
            total += jnp.dot(own_ref[index], coef_ref[b, k], preferred_element_type=F32)
        acc_ref[:, lanes] = total


def own_kernel(cols_ref, state_ref, tangent_ref, coef_ref, rate_ref, coupling_ref, acc_ref, own_ref, *, block):
    own_terms(
        cols_ref, state_ref, tangent_ref, coef_ref, rate_ref, coupling_ref, acc_ref, own_ref, block, lambda b: None
    )


def load_kernel(
    cols_ref, state_ref, tangent_ref, rate_ref, coupling_ref, coef_hbm, implicit_hbm,
    acc_ref, coef_ref, implicit_ref, own_ref, sems, *, block,
):
    blocks = coef_ref.shape[0]
    chunk = 4
    parts = [slice(b, min(b + chunk, blocks)) for b in range(0, blocks, chunk)]
    copies = start_copies([coef_hbm.at[part] for part in parts], [coef_ref.at[part] for part in parts], sems)
    copies += start_copies((implicit_hbm,), (implicit_ref,), sems, blocks)
    own_terms(
        cols_ref, state_ref, tangent_ref, coef_ref, rate_ref, coupling_ref, acc_ref, own_ref, block,
        lambda b: copies[b // chunk].wait() if b % chunk == 0 else None,
    )
    copies[-1].wait()


def halo_blocks(meta_ref, recvs, halo_ref, halo):
    channels = halo_ref.shape[1]
    for at, recv in enumerate(recvs):
        for s in range(halo):
            piece = recv[s * channels : (s + 1) * channels, :]
            if at == 1:
                piece = jnp.where(meta_ref[2] > 0, jnp.zeros_like(piece), piece)
            halo_ref[at * halo + s] = piece


def transported(cols_ref, meta_ref, acc_ref, coef_ref, halo_ref, explicit_ref, halo, block):
    blocks = coef_ref.shape[0]
    lat_odd = meta_ref[0] % 2
    lon_odd = meta_ref[1] % 2
    shifts = (1 - lat_odd, lat_odd, 3 - lon_odd, 2 + lon_odd)
    offsets = [shifts[d] * halo - (blocks + d * halo) for d in range(4)]
    for b in range(blocks):
        pieces = [halo_ref[offsets[d] + cols_ref[1 + d, b]] for d in range(4)]
        gathered = jnp.concatenate(pieces, axis=1)
        weights = coef_ref[b, 1:5].reshape(4 * block, block)
        moved = jnp.dot(gathered, weights, preferred_element_type=F32)
        explicit_ref[b] = (acc_ref[:, b * block : (b + 1) * block] + moved).astype(BF16)


def step_kernel(
    cols_ref, meta_ref, sends_ref, acc_ref, a_ref, b_ref, c_ref, r_ref, coef_ref, implicit_ref,
    state_ref, tangent_ref, a_out, b_out, c_out, r_out, halo_ref, explicit_ref, own_ref, *, halo, block,
):
    halo_blocks(meta_ref, (a_ref, b_ref, c_ref, r_ref), halo_ref, halo)
    tracers = state_ref.shape[0]
    transported(cols_ref, meta_ref, acc_ref, coef_ref, halo_ref, explicit_ref, halo, block)
    for b in range(coef_ref.shape[0]):
        lanes = slice(b * block, (b + 1) * block)
        new = jnp.dot(explicit_ref[b], implicit_ref[b], preferred_element_type=F32)
        state_ref[:, lanes] = new[:tracers]
        tangent_ref[:, lanes] = new[tracers:]
        own_ref[b] = new.astype(BF16)
    pick_sends(sends_ref, meta_ref, lambda index: own_ref[index], (a_out, b_out, c_out, r_out), halo)


def last_kernel(
    cols_ref, meta_ref, acc_ref, a_ref, b_ref, c_ref, r_ref, coef_ref, implicit_ref, start_ref, region_ref,
    state_ref, residual_ref, totals_ref, halo_ref, explicit_ref, both_ref, *, halo, block, row_regions,
):
    halo_blocks(meta_ref, (a_ref, b_ref, c_ref, r_ref), halo_ref, halo)
    tracers, rows = state_ref.shape
    first = meta_ref[0] * row_regions
    transported(cols_ref, meta_ref, acc_ref, coef_ref, halo_ref, explicit_ref, halo, block)
    for b in range(coef_ref.shape[0]):
        lanes = slice(b * block, (b + 1) * block)
        new = jnp.dot(explicit_ref[b], implicit_ref[b], preferred_element_type=F32)
        state_ref[:, lanes] = new[:tracers]
        residual = new[tracers:] - start_ref[:, lanes]
        residual_ref[:, lanes] = residual
        high, low = split2(residual)
        both_ref[:tracers, lanes] = high
        both_ref[tracers:, lanes] = low
    ids = lax.broadcasted_iota(jnp.int32, (row_regions, rows), 0) + first
    chosen = (ids == region_ref[...]).astype(F32).astype(BF16)
    sums = lax.dot_general(both_ref[...], chosen, (((1,), (1,)), ((), ())), preferred_element_type=F32)
    sums = sums[:tracers] + sums[tracers:]
    width = totals_ref.shape[1]
    if width > row_regions:
        sums = jnp.concatenate([sums, jnp.zeros((tracers, width - row_regions), F32)], axis=1)
    totals_ref[...] = pltpu.roll(sums, first, 1)


def correct_kernel(
    meta_ref, totals_ref, inverse_ref, c_ref, r_ref, region_ref, residual_ref, out_ref, *, skip, block
):
    regions, width = inverse_ref.shape
    tracers = totals_ref.shape[0]
    t_high, t_low = split2(totals_ref[...])
    both = jnp.concatenate([t_high, t_low], axis=0)
    values = jnp.zeros((tracers, 3 * regions), F32)
    nt = (((1,), (1,)), ((), ()))
    for at in range(width // block):
        lanes = slice(at * block, (at + 1) * block)
        rows = slice(skip + at * 2 * regions, skip + (at + 1) * 2 * regions)
        own_high, own_low = split2(inverse_ref[:, lanes])
        c_all = c_ref[rows, :].astype(F32)
        r_all = r_ref[rows, :].astype(F32)
        high = jnp.concatenate([own_high.astype(F32), c_all[:regions], r_all[:regions]], axis=0).astype(BF16)
        low = jnp.concatenate([own_low.astype(F32), c_all[regions:], r_all[regions:]], axis=0).astype(BF16)
        part = lax.dot_general(both[:, lanes], high, nt, preferred_element_type=F32)
        values += part[:tracers] + part[tracers:]
        values += lax.dot_general(t_high[:, lanes], low, nt, preferred_element_type=F32)
    v_high, v_low = split2(values)
    rows_id = lax.broadcasted_iota(jnp.int32, (3 * regions, 1), 0)
    group = rows_id // regions
    base = jnp.where(group == 0, meta_ref[3], jnp.where(group == 1, meta_ref[4], meta_ref[5]))
    ids = base * regions + rows_id % regions
    chosen = (ids == region_ref[...]).astype(F32).astype(BF16)
    out = jnp.dot(v_high, chosen, preferred_element_type=F32)
    out += jnp.dot(v_low, chosen, preferred_element_type=F32)
    out_ref[...] = residual_ref[...] + out


def partners(n_lat, n_lon):
    def flat(la, lo):
        return la * n_lon + lo

    lat_even, lat_odd, core, ring = [], [], [], []
    for la in range(n_lat):
        for lo in range(n_lon):
            me = flat(la, lo)
            lat_even.append((me, flat(la ^ 1, lo)))
            if la in (0, n_lat - 1):
                lat_odd.append((me, flat(la, lo ^ 1)))
            else:
                lat_odd.append((me, flat(la + 1 if la % 2 else la - 1, lo)))
            core.append((me, flat(la, lo ^ 1)))
            ring.append((me, flat(la, (lo + 1 if lo % 2 else lo - 1) % n_lon)))
    return lat_even, lat_odd, core, ring


def local(
    state_init, tangent_init, coef_blocks, column_lists, send_lists, implicit_blocks,
    uptake_rate, coupling, region_map, coarse_inverse,
):
    n_lat, n_lon = lax.axis_size("lat"), lax.axis_size("lon")
    tracers, rows = state_init.shape
    blocks, entries, block = coef_blocks.shape[:3]
    halo = send_lists.shape[2]
    channels = 2 * tracers
    regions, width = coarse_inverse.shape
    devices = n_lat * n_lon
    lat_pos, lon_pos = lax.axis_index("lat"), lax.axis_index("lon")
    edge = ((lat_pos == 0) | (lat_pos == n_lat - 1)).astype(jnp.int32)
    ring_lon = (lon_pos + jnp.where(lon_pos % 2 == 0, n_lon - 1, 1)) % n_lon
    base = lat_pos * n_lon
    meta = jnp.stack([lat_pos, lon_pos, edge, base + lon_pos, base + (lon_pos ^ 1), base + ring_lon])
    meta = meta.astype(jnp.int32)
    sends = send_lists[0].T
    cols = column_lists.T
    rate = uptake_rate.reshape(1, rows)
    region = region_map.reshape(1, rows)
    perms = partners(n_lat, n_lon)

    halo_shape = jax.ShapeDtypeStruct((halo * channels, block), BF16)
    lon_shape = jax.ShapeDtypeStruct((halo * channels + 2 * regions * (width // block), block), BF16)
    field = jax.ShapeDtypeStruct((tracers, rows), F32)
    acc_shape = jax.ShapeDtypeStruct((channels, rows), F32)
    like = lambda value: jax.ShapeDtypeStruct(value.shape, value.dtype)
    halo_scratch = pltpu.VMEM((4 * halo, channels, block), BF16)
    block_scratch = pltpu.VMEM((blocks, channels, block), BF16)
    own_scratch = pltpu.VMEM((blocks + 1, channels, block), BF16)
    dma = pltpu.SemaphoreType.DMA

    def call(kernel, name, outs, n_smem, n_vmem, n_any, scratch, flops=0, **static):
        return pl.pallas_call(
            functools.partial(kernel, block=block, **static),
            out_shape=outs,
            in_specs=smem(n_smem) + vmem(n_vmem) + [pl.BlockSpec(memory_space=pltpu.HBM)] * n_any,
            out_specs=jax.tree.map(lambda _: vmem(1)[0], outs),
            scratch_shapes=scratch,
            compiler_params=params(),
            cost_estimate=pl.CostEstimate(flops=flops, bytes_accessed=10**6, transcendentals=0),
            name=name,
        )

    smalls = (state_init, tangent_init, coarse_inverse, cols, rate, coupling, region)
    first = call(
        first_kernel, "first",
        (halo_shape, halo_shape, lon_shape, lon_shape) + tuple(like(v) for v in smalls) + (like(sends),),
        1, 0, 8, [pltpu.SMEM(sends.shape, jnp.int32), dma((9,))], halo=halo,
    )
    load = call(
        load_kernel, "load", (acc_shape, like(coef_blocks), like(implicit_blocks)), 1, 4, 2,
        [own_scratch, dma((blocks + 1,))], flops=10**9,
    )
    own = call(own_kernel, "own", acc_shape, 1, 5, 0, [own_scratch], flops=10**9)
    step = call(
        step_kernel, "step", (field, field) + (halo_shape,) * 4, 3, 7, 0,
        [halo_scratch, block_scratch, block_scratch], halo=halo,
    )
    last = call(
        last_kernel, "last", (field, field, jax.ShapeDtypeStruct((tracers, width), F32)), 2, 9, 0,
        [halo_scratch, block_scratch, pltpu.VMEM((channels, rows), BF16)],
        halo=halo, row_regions=n_lon * regions,
    )
    correct = call(correct_kernel, "correct", field, 1, 6, 0, [], skip=halo * channels)

    def exchange(sent):
        return [lax.ppermute(value, BOTH, pairs) for value, pairs in zip(sent, perms)]

    far = lambda value: pltpu.with_memory_space_constraint(value, pltpu.HBM)
    *sent, state, start, inverse, cols, rate, coupling, region, sends = first(
        meta, *map(far, (sends, state_init, tangent_init, coarse_inverse, cols, rate, coupling, region))
    )
    got1 = exchange(sent)
    acc, coef, implicit = load(cols, state, start, rate, coupling, far(coef_blocks), far(implicit_blocks))
    state, tangent, *sent = step(cols, meta, sends, acc, *got1, coef, implicit)
    got2 = exchange(sent)
    acc = own(cols, state, tangent, coef, rate, coupling)
    final_state, residual, totals = last(cols, meta, acc, *got2, coef, implicit, start, region)
    bit = 1
    while bit < devices:
        mask = bit | 1
        totals = totals + lax.ppermute(totals, BOTH, [(i, i ^ mask) for i in range(devices)])
        bit *= 2
    preconditioned = correct(meta, totals, inverse, got1[2], got1[3], region, residual)
    return final_state, preconditioned


def solution(mesh):
    placed = (
        P(None, BOTH),
        P(None, BOTH),
        P(BOTH, None, None, None),
        P(BOTH, None),
        P(BOTH, None, None),
        P(BOTH, None, None),
        P(BOTH),
        P(),
        P(BOTH),
        P(BOTH, None),
    )
    return jax.shard_map(
        local,
        mesh=mesh,
        in_specs=placed,
        out_specs=(P(None, BOTH), P(None, BOTH)),
        check_vma=False,
    )
```

```python
import functools

import jax
import jax.numpy as jnp
from jax import lax
from jax.experimental import pallas as pl
from jax.experimental.pallas import tpu as pltpu
from jax.sharding import PartitionSpec as P

BOTH = ("lat", "lon")
F32 = jnp.float32
BF16 = jnp.bfloat16
step_length = 0.5


def split2(value):
    high = value.astype(BF16)
    low = (value - high.astype(F32)).astype(BF16)
    return high, low


def vmem(count):
    return [pl.BlockSpec(memory_space=pltpu.VMEM)] * count


def smem(count):
    return [pl.BlockSpec(memory_space=pltpu.SMEM)] * count


def params():
    return pltpu.CompilerParams(vmem_limit_bytes=24 * 1024 * 1024)


def pick_sends(sends_ref, meta_ref, rounded_of, outs, halo):
    lat_odd = meta_ref[0] % 2
    lon_odd = meta_ref[1] % 2
    lists = (lat_odd, 1 - lat_odd, 2 + lon_odd, 3 - lon_odd)
    for out_ref, which in zip(outs, lists):
        for at in range(halo):
            piece = rounded_of(sends_ref[at, which])
            out_ref[at * piece.shape[0] : (at + 1) * piece.shape[0], :] = piece


def start_copies(sources, targets, sems, base=0):
    copies = []
    for at, (source, target) in enumerate(zip(sources, targets)):
        copy = pltpu.make_async_copy(source, target, sems.at[base + at])
        copy.start()
        copies.append(copy)
    return copies


def prelude_kernel(
    meta_ref, sends_hbm, state_hbm, tangent_hbm, inverse_hbm, cols_hbm, rate_hbm, coupling_hbm, region_hbm,
    coef_hbm, implicit_hbm,
    a_out, b_out, c_out, r_out, state_ref, tangent_ref, inverse_ref, cols_out, rate_ref, coupling_ref, region_ref,
    sends_out, coef_ref, implicit_ref, m_ref,
    sends_ref, cols_ref, share_ref, sems, *, halo, block, row_regions, chunk,
):
    blocks = coef_ref.shape[0]
    parts = [slice(b, min(b + chunk, blocks)) for b in range(0, blocks, chunk)]
    sources = (
        [sends_hbm, cols_hbm, region_hbm, state_hbm, tangent_hbm, inverse_hbm, implicit_hbm]
        + [coef_hbm.at[part] for part in parts]
        + [cols_hbm, rate_hbm, coupling_hbm, sends_hbm]
    )
    targets = (
        [sends_ref, cols_ref, region_ref, state_ref, tangent_ref, inverse_ref, implicit_ref]
        + [coef_ref.at[part] for part in parts]
        + [cols_out, rate_ref, coupling_ref, sends_out]
    )
    copies = start_copies(sources, targets, sems)
    for copy in copies[:6]:
        copy.wait()

    def rounded_of(index):
        lanes = pl.ds(pl.multiple_of(index * block, block), block)
        return jnp.concatenate([state_ref[:, lanes], tangent_ref[:, lanes]], axis=0).astype(BF16)

    outs = (a_out, b_out, c_out, r_out)
    pick_sends(sends_ref, meta_ref, rounded_of, outs, halo)
    channels = 2 * state_ref.shape[0]
    regions, width = inverse_ref.shape
    for at in range(width // block):
        high, low = split2(inverse_ref[:, at * block : (at + 1) * block])
        piece = jnp.concatenate([high.astype(F32), low.astype(F32)], axis=0).astype(BF16)
        start = halo * (channels + row_regions) + at * 2 * regions
        for out_ref in outs[2:]:
            out_ref[start : start + 2 * regions, :] = piece
    share_ref[...] = jnp.zeros_like(share_ref)
    copies[6].wait()
    nt = (((1,), (1,)), ((), ()))
    ids = lax.broadcasted_iota(jnp.int32, (row_regions, block), 0) + meta_ref[0] * row_regions
    for b in range(blocks):
        lanes = slice(b * block, (b + 1) * block)
        chosen = (ids == region_ref[:, lanes]).astype(F32).astype(BF16)
        high, low = split2(lax.dot_general(chosen, implicit_ref[b], nt, preferred_element_type=F32))
        m_ref[:row_regions, lanes] = high
        m_ref[row_regions:, lanes] = low
    offsets = slot_offsets(meta_ref, blocks, halo)
    for b in range(blocks):
        if b % chunk == 0:
            copies[7 + b // chunk].wait()
        lanes = slice(b * block, (b + 1) * block)
        weights = coef_ref[b, 1:5].reshape(4 * block, block)
        part = lax.dot_general(m_ref[:row_regions, lanes], weights, nt, preferred_element_type=F32)
        for d in range(4):
            slot = offsets[d] + cols_ref[1 + d, b]
            share_ref[slot] += part[:, d * block : (d + 1) * block]
    for at, out_ref in enumerate(outs):
        for s in range(halo):
            start = halo * channels + s * row_regions
            out_ref[start : start + row_regions, :] = share_ref[at * halo + s].astype(BF16)
    for copy in copies[7 + len(parts) :]:
        copy.wait()


def own_terms(cols_ref, state_ref, tangent_ref, coef_ref, rate_ref, coupling_ref, acc_ref, own_ref, block):
    tracers = state_ref.shape[0]
    blocks, entries = coef_ref.shape[:2]
    own_ref[blocks] = jnp.zeros(own_ref.shape[1:], BF16)
    high, low = split2(coupling_ref[...] * step_length)
    zero = jnp.zeros_like(high)
    mix_high = jnp.concatenate(
        [jnp.concatenate([high, zero], axis=1), jnp.concatenate([zero, high], axis=1)], axis=0
    )
    mix_low = jnp.concatenate(
        [jnp.concatenate([low, zero], axis=1), jnp.concatenate([zero, low], axis=1)], axis=0
    )
    mix = jnp.concatenate([mix_high, mix_high, mix_low], axis=1)
    for b in range(blocks):
        lanes = slice(b * block, (b + 1) * block)
        state = state_ref[:, lanes]
        tangent = tangent_ref[:, lanes]
        rate = rate_ref[:, lanes]
        squared = state * state
        inverse = 1.0 / (1.0 + squared)
        scaled = rate * inverse
        uptake = scaled * state
        slope = scaled * inverse * (1.0 - squared) * tangent
        term_high, term_low = split2(jnp.concatenate([uptake, slope], axis=0))
        terms = jnp.concatenate([term_high, term_low, term_high], axis=0)
        stacked = jnp.concatenate([state, tangent], axis=0)
        own_ref[b] = stacked.astype(BF16)
        acc_ref[:, lanes] = stacked + jnp.dot(mix, terms, preferred_element_type=F32)
    for b in range(blocks):
        lanes = slice(b * block, (b + 1) * block)
        total = acc_ref[:, lanes] + jnp.dot(own_ref[b], coef_ref[b, 0], preferred_element_type=F32)
        for k in range(5, entries):
            index = jnp.minimum(cols_ref[k, b], blocks)
            total += jnp.dot(own_ref[index], coef_ref[b, k], preferred_element_type=F32)
        acc_ref[:, lanes] = total


def own_kernel(cols_ref, state_ref, tangent_ref, coef_ref, rate_ref, coupling_ref, acc_ref, own_ref, *, block):
    own_terms(cols_ref, state_ref, tangent_ref, coef_ref, rate_ref, coupling_ref, acc_ref, own_ref, block)


def slot_offsets(meta_ref, blocks, halo):
    lat_odd = meta_ref[0] % 2
    lon_odd = meta_ref[1] % 2
    shifts = (1 - lat_odd, lat_odd, 3 - lon_odd, 2 + lon_odd)
    return [shifts[d] * halo - (blocks + d * halo) for d in range(4)]


def halo_blocks(meta_ref, recvs, halo_ref, halo):
    channels = halo_ref.shape[1]
    for at, recv in enumerate(recvs):
        for s in range(halo):
            piece = recv[s * channels : (s + 1) * channels, :]
            if at == 1:
                piece = jnp.where(meta_ref[2] > 0, jnp.zeros_like(piece), piece)
            halo_ref[at * halo + s] = piece.astype(BF16)


def transported(cols_ref, meta_ref, acc_ref, coef_ref, halo_ref, explicit_ref, halo, block):
    blocks = coef_ref.shape[0]
    offsets = slot_offsets(meta_ref, blocks, halo)
    for b in range(blocks):
        pieces = [halo_ref[offsets[d] + cols_ref[1 + d, b]] for d in range(4)]
        gathered = jnp.concatenate(pieces, axis=1)
        weights = coef_ref[b, 1:5].reshape(4 * block, block)
        moved = jnp.dot(gathered, weights, preferred_element_type=F32)
        explicit_ref[b] = (acc_ref[:, b * block : (b + 1) * block] + moved).astype(BF16)


def step_kernel(
    cols_ref, meta_ref, sends_ref, acc_ref, a_ref, b_ref, c_ref, r_ref, coef_ref, implicit_ref, rate_ref, coupling_ref,
    start_ref, region_ref, m_ref,
    a_out, b_out, c_out, r_out, next_ref, totals_ref, halo_ref, explicit_ref, own_ref, state_ref, tangent_ref, both_ref,
    *, halo, block, row_regions, n_lat,
):
    recvs = (a_ref, b_ref, c_ref, r_ref)
    outs = (a_out, b_out, c_out, r_out)
    halo_blocks(meta_ref, recvs, halo_ref, halo)
    tracers, rows = state_ref.shape
    channels = 2 * tracers
    blocks = coef_ref.shape[0]
    transported(cols_ref, meta_ref, acc_ref, coef_ref, halo_ref, explicit_ref, halo, block)
    for b in range(blocks):
        lanes = slice(b * block, (b + 1) * block)
        new = jnp.dot(explicit_ref[b], implicit_ref[b], preferred_element_type=F32)
        state_ref[:, lanes] = new[:tracers]
        tangent_ref[:, lanes] = new[tracers:]
        own_ref[b] = new.astype(BF16)
    pick_sends(sends_ref, meta_ref, lambda index: own_ref[index].astype(a_out.dtype), outs, halo)
    own_terms(cols_ref, state_ref, tangent_ref, coef_ref, rate_ref, coupling_ref, next_ref, own_ref, block)

    nt = (((1,), (1,)), ((), ()))
    high, low = split2(next_ref[tracers:, :])
    both_ref[:tracers, :] = high
    both_ref[tracers:, :] = low
    m_high = m_ref[:row_regions, :]
    sums = lax.dot_general(both_ref[...], m_high, nt, preferred_element_type=F32)
    sums = sums[:tracers] + sums[tracers:]
    sums += lax.dot_general(high, m_ref[row_regions:, :], nt, preferred_element_type=F32)
    ids = lax.broadcasted_iota(jnp.int32, (row_regions, rows), 0) + meta_ref[0] * row_regions
    chosen = (ids == region_ref[...]).astype(F32).astype(BF16)
    high, low = split2(start_ref[...])
    both_ref[:tracers, :] = high
    both_ref[tracers:, :] = low
    begun = lax.dot_general(both_ref[...], chosen, nt, preferred_element_type=F32)
    sums -= begun[:tracers] + begun[tracers:]

    shares = []
    for at in range(4):
        share = jnp.zeros((tracers, row_regions), F32)
        for s in range(halo):
            piece = outs[at][s * channels + tracers : (s + 1) * channels, :].astype(BF16)
            start = halo * channels + s * row_regions
            weights = recvs[at][start : start + row_regions, :]
            share += lax.dot_general(piece, weights, nt, preferred_element_type=F32)
        shares.append(share)
    lat = meta_ref[0]
    shares[1] = jnp.where(meta_ref[2] > 0, jnp.zeros_like(shares[1]), shares[1])
    row_a = lat + 1 - 2 * (lat % 2)
    row_b = jnp.where(meta_ref[2] > 0, lat, lat - 1 + 2 * (lat % 2))
    width = totals_ref.shape[0] // tracers * block

    def placed(value, row):
        if width > row_regions:
            value = jnp.concatenate([value, jnp.zeros((tracers, width - row_regions), F32)], axis=1)
        return pltpu.roll(value, row * row_regions, 1)

    total = placed(sums + shares[2] + shares[3], lat) + placed(shares[0], row_a) + placed(shares[1], row_b)
    for at in range(width // block):
        totals_ref[at * tracers : (at + 1) * tracers, :] = total[:, at * block : (at + 1) * block]


def last_kernel(
    cols_ref, meta_ref, acc_ref, a_ref, b_ref, c_ref, r_ref, coef_ref, implicit_ref, start_ref,
    state_ref, residual_ref, halo_ref, explicit_ref, *, halo, block,
):
    halo_blocks(meta_ref, (a_ref, b_ref, c_ref, r_ref), halo_ref, halo)
    tracers, rows = state_ref.shape
    transported(cols_ref, meta_ref, acc_ref, coef_ref, halo_ref, explicit_ref, halo, block)
    for b in range(coef_ref.shape[0]):
        lanes = slice(b * block, (b + 1) * block)
        new = jnp.dot(explicit_ref[b], implicit_ref[b], preferred_element_type=F32)
        state_ref[:, lanes] = new[:tracers]
        residual_ref[:, lanes] = new[tracers:] - start_ref[:, lanes]


def correct_kernel(
    meta_ref, totals_ref, inverse_ref, c_ref, r_ref, region_ref, residual_ref, out_ref, *, skip, block
):
    regions, width = inverse_ref.shape
    tracers = residual_ref.shape[0]
    values = jnp.zeros((tracers, 3 * regions), F32)
    nt = (((1,), (1,)), ((), ()))
    for at in range(width // block):
        t_high, t_low = split2(totals_ref[at * tracers : (at + 1) * tracers, :])
        both = jnp.concatenate([t_high, t_low], axis=0)
        lanes = slice(at * block, (at + 1) * block)
        rows = slice(skip + at * 2 * regions, skip + (at + 1) * 2 * regions)
        own_high, own_low = split2(inverse_ref[:, lanes])
        c_all = c_ref[rows, :].astype(F32)
        r_all = r_ref[rows, :].astype(F32)
        high = jnp.concatenate([own_high.astype(F32), c_all[:regions], r_all[:regions]], axis=0).astype(BF16)
        low = jnp.concatenate([own_low.astype(F32), c_all[regions:], r_all[regions:]], axis=0).astype(BF16)
        part = lax.dot_general(both, high, nt, preferred_element_type=F32)
        values += part[:tracers] + part[tracers:]
        values += lax.dot_general(t_high, low, nt, preferred_element_type=F32)
    v_high, v_low = split2(values)
    rows_id = lax.broadcasted_iota(jnp.int32, (3 * regions, 1), 0)
    group = rows_id // regions
    base = jnp.where(group == 0, meta_ref[3], jnp.where(group == 1, meta_ref[4], meta_ref[5]))
    ids = base * regions + rows_id % regions
    chosen = (ids == region_ref[...]).astype(F32).astype(BF16)
    out = jnp.dot(v_high, chosen, preferred_element_type=F32)
    out += jnp.dot(v_low, chosen, preferred_element_type=F32)
    out_ref[...] = residual_ref[...] + out


def partners(n_lat, n_lon):
    def flat(la, lo):
        return la * n_lon + lo

    lat_even, lat_odd, core, ring = [], [], [], []
    for la in range(n_lat):
        for lo in range(n_lon):
            me = flat(la, lo)
            lat_even.append((me, flat(la ^ 1, lo)))
            if la in (0, n_lat - 1):
                lat_odd.append((me, flat(la, lo ^ 1)))
            else:
                lat_odd.append((me, flat(la + 1 if la % 2 else la - 1, lo)))
            core.append((me, flat(la, lo ^ 1)))
            ring.append((me, flat(la, (lo + 1 if lo % 2 else lo - 1) % n_lon)))
    return lat_even, lat_odd, core, ring


def local(
    state_init, tangent_init, coef_blocks, column_lists, send_lists, implicit_blocks,
    uptake_rate, coupling, region_map, coarse_inverse,
):
    n_lat, n_lon = lax.axis_size("lat"), lax.axis_size("lon")
    tracers, rows = state_init.shape
    blocks, entries, block = coef_blocks.shape[:3]
    halo = send_lists.shape[2]
    channels = 2 * tracers
    regions, width = coarse_inverse.shape
    devices = n_lat * n_lon
    lat_pos, lon_pos = lax.axis_index("lat"), lax.axis_index("lon")
    edge = ((lat_pos == 0) | (lat_pos == n_lat - 1)).astype(jnp.int32)
    ring_lon = (lon_pos + jnp.where(lon_pos % 2 == 0, n_lon - 1, 1)) % n_lon
    base = lat_pos * n_lon
    meta = jnp.stack([lat_pos, lon_pos, edge, base + lon_pos, base + (lon_pos ^ 1), base + ring_lon])
    meta = meta.astype(jnp.int32)
    sends = send_lists[0].T
    cols = column_lists.T
    rate = uptake_rate.reshape(1, rows)
    region = region_map.reshape(1, rows)
    perms = partners(n_lat, n_lon)
    row_regions = n_lon * regions
    shared = halo * (channels + row_regions)
    lat_shape = jax.ShapeDtypeStruct((shared, block), BF16)
    lon_shape = jax.ShapeDtypeStruct((shared + 2 * regions * (width // block), block), BF16)
    halo_shape = jax.ShapeDtypeStruct((halo * channels, block), F32)
    totals_shape = jax.ShapeDtypeStruct((tracers * (width // block), block), F32)
    field = jax.ShapeDtypeStruct((tracers, rows), F32)
    acc_shape = jax.ShapeDtypeStruct((channels, rows), F32)
    like = lambda value: jax.ShapeDtypeStruct(value.shape, value.dtype)
    halo_scratch = pltpu.VMEM((4 * halo, channels, block), BF16)
    block_scratch = pltpu.VMEM((blocks, channels, block), BF16)
    own_scratch = pltpu.VMEM((blocks + 1, channels, block), BF16)
    field_scratch = pltpu.VMEM((tracers, rows), F32)
    dma = pltpu.SemaphoreType.DMA
    chunk = 4

    def call(kernel, name, outs, n_smem, n_vmem, n_any, scratch, flops=0, **static):
        return pl.pallas_call(
            functools.partial(kernel, block=block, **static),
            out_shape=outs,
            in_specs=smem(n_smem) + vmem(n_vmem) + [pl.BlockSpec(memory_space=pltpu.HBM)] * n_any,
            out_specs=jax.tree.map(lambda _: vmem(1)[0], outs),
            scratch_shapes=scratch,
            compiler_params=params(),
            cost_estimate=pl.CostEstimate(flops=flops, bytes_accessed=10**6, transcendentals=0),
            name=name,
        )

    far = lambda value: pltpu.with_memory_space_constraint(value, pltpu.HBM)
    smalls = (state_init, tangent_init, coarse_inverse, cols, rate, coupling, region)
    prelude = call(
        prelude_kernel, "prelude",
        (lat_shape, lat_shape, lon_shape, lon_shape)
        + tuple(like(v) for v in smalls + (sends, coef_blocks, implicit_blocks))
        + (jax.ShapeDtypeStruct((2 * row_regions, rows), BF16),),
        1, 0, 10,
        [
            pltpu.SMEM(sends.shape, jnp.int32),
            pltpu.SMEM(cols.shape, jnp.int32),
            pltpu.VMEM((4 * halo, row_regions, block), F32),
            dma((11 + -(-blocks // chunk),)),
        ],
        halo=halo, row_regions=row_regions, chunk=chunk,
    )
    own = call(own_kernel, "own", acc_shape, 1, 5, 0, [own_scratch], flops=10**9)
    step = call(
        step_kernel, "step", (halo_shape,) * 4 + (acc_shape, totals_shape), 3, 12, 0,
        [halo_scratch, block_scratch, own_scratch, field_scratch, field_scratch, pltpu.VMEM((channels, rows), BF16)],
        halo=halo, row_regions=row_regions, n_lat=n_lat,
    )
    last = call(last_kernel, "last", (field, field), 2, 8, 0, [halo_scratch, block_scratch], flops=10**9, halo=halo)
    correct = call(correct_kernel, "correct", field, 1, 6, 0, [], skip=shared)

    *sent, state, start, inverse, cols, rate, coupling, region, sends, coef, implicit, folded = prelude(
        meta, *map(far, (sends, *smalls, coef_blocks, implicit_blocks))
    )
    got1 = [lax.ppermute(value, BOTH, pairs) for value, pairs in zip(sent, perms)]
    acc = own(cols, state, start, coef, rate, coupling)
    *sent, acc, totals = step(
        cols, meta, sends, acc, *got1, coef, implicit, rate, coupling, start, region, folded
    )
    got2 = [None] * 4
    bit = 1
    while bit < devices:
        options = [[(i, i ^ mask) for i in range(devices)] for mask in (bit | 1, bit)]
        shared_with = [(at, pairs) for pairs in options for at in range(4) if perms[at] == pairs and got2[at] is None]
        if shared_with:
            at, pairs = shared_with[0]
            got2[at] = lax.ppermute(jnp.concatenate([sent[at], totals], axis=0), BOTH, pairs)
            totals = totals + got2[at][halo * channels :]
        else:
            totals = totals + lax.ppermute(totals, BOTH, options[0])
        bit *= 2
    for at in range(4):
        if got2[at] is None:
            got2[at] = lax.ppermute(sent[at].astype(BF16), BOTH, perms[at])
    final_state, residual = last(cols, meta, acc, *got2, coef, implicit, start)
    preconditioned = correct(meta, totals, inverse, got1[2], got1[3], region, residual)
    return final_state, preconditioned


def solution(mesh):
    placed = (
        P(None, BOTH),
        P(None, BOTH),
        P(BOTH, None, None, None),
        P(BOTH, None),
        P(BOTH, None, None),
        P(BOTH, None, None),
        P(BOTH),
        P(),
        P(BOTH),
        P(BOTH, None),
    )
    return jax.shard_map(
        local,
        mesh=mesh,
        in_specs=placed,
        out_specs=(P(None, BOTH), P(None, BOTH)),
        check_vma=False,
    )
```

```python
import functools

import jax
import jax.numpy as jnp
from jax import lax
from jax.experimental import pallas as pl
from jax.experimental.pallas import tpu as pltpu
from jax.sharding import PartitionSpec as P

BOTH = ("lat", "lon")
F32 = jnp.float32
BF16 = jnp.bfloat16
step_length = 0.5


def split2(value):
    high = value.astype(BF16)
    low = (value - high.astype(F32)).astype(BF16)
    return high, low


def vmem(count):
    return [pl.BlockSpec(memory_space=pltpu.VMEM)] * count


def smem(count):
    return [pl.BlockSpec(memory_space=pltpu.SMEM)] * count


def params():
    return pltpu.CompilerParams(vmem_limit_bytes=24 * 1024 * 1024)


def pick_sends(sends_ref, meta_ref, rounded_of, outs, halo):
    lat_odd = meta_ref[0] % 2
    lon_odd = meta_ref[1] % 2
    lists = (lat_odd, 1 - lat_odd, 2 + lon_odd, 3 - lon_odd)
    for out_ref, which in zip(outs, lists):
        for at in range(halo):
            piece = rounded_of(sends_ref[at, which])
            out_ref[at * piece.shape[0] : (at + 1) * piece.shape[0], :] = piece


def start_copies(sources, targets, sems, base=0):
    copies = []
    for at, (source, target) in enumerate(zip(sources, targets)):
        copy = pltpu.make_async_copy(source, target, sems.at[base + at])
        copy.start()
        copies.append(copy)
    return copies


def prelude_kernel(
    meta_ref, sends_hbm, state_hbm, tangent_hbm, inverse_hbm, cols_hbm, rate_hbm, coupling_hbm, region_hbm,
    coef_hbm, implicit_hbm,
    a_out, b_out, c_out, r_out, state_ref, tangent_ref, inverse_ref, cols_out, rate_ref, coupling_ref, region_ref,
    sends_out, coef_ref, implicit_ref, m_ref,
    sends_ref, cols_ref, share_ref, sems, *, halo, block, row_regions, chunk,
):
    blocks = coef_ref.shape[0]
    parts = [slice(b, min(b + chunk, blocks)) for b in range(0, blocks, chunk)]
    sources = (
        [sends_hbm, cols_hbm, region_hbm, state_hbm, tangent_hbm, inverse_hbm, implicit_hbm]
        + [coef_hbm.at[part, 1:5] for part in parts]
        + [cols_hbm, rate_hbm, coupling_hbm, sends_hbm]
    )
    targets = (
        [sends_ref, cols_ref, region_ref, state_ref, tangent_ref, inverse_ref, implicit_ref]
        + [coef_ref.at[part] for part in parts]
        + [cols_out, rate_ref, coupling_ref, sends_out]
    )
    copies = start_copies(sources, targets, sems)
    for copy in copies[:6]:
        copy.wait()

    def rounded_of(index):
        lanes = pl.ds(pl.multiple_of(index * block, block), block)
        return jnp.concatenate([state_ref[:, lanes], tangent_ref[:, lanes]], axis=0).astype(BF16)

    outs = (a_out, b_out, c_out, r_out)
    pick_sends(sends_ref, meta_ref, rounded_of, outs, halo)
    channels = 2 * state_ref.shape[0]
    regions, width = inverse_ref.shape
    for at in range(width // block):
        high, low = split2(inverse_ref[:, at * block : (at + 1) * block])
        piece = jnp.concatenate([high.astype(F32), low.astype(F32)], axis=0).astype(BF16)
        start = halo * (channels + row_regions) + at * 2 * regions
        for out_ref in outs[2:]:
            out_ref[start : start + 2 * regions, :] = piece
    share_ref[...] = jnp.zeros_like(share_ref)
    copies[6].wait()
    nt = (((1,), (1,)), ((), ()))
    ids = lax.broadcasted_iota(jnp.int32, (row_regions, block), 0) + meta_ref[0] * row_regions
    for b in range(blocks):
        lanes = slice(b * block, (b + 1) * block)
        chosen = (ids == region_ref[:, lanes]).astype(F32).astype(BF16)
        high, low = split2(lax.dot_general(chosen, implicit_ref[b], nt, preferred_element_type=F32))
        m_ref[:row_regions, lanes] = high
        m_ref[row_regions:, lanes] = low
    offsets = slot_offsets(meta_ref, blocks, halo)
    for b in range(blocks):
        if b % chunk == 0:
            copies[7 + b // chunk].wait()
        lanes = slice(b * block, (b + 1) * block)
        weights = coef_ref[b].reshape(4 * block, block)
        part = lax.dot_general(m_ref[:row_regions, lanes], weights, nt, preferred_element_type=F32)
        for d in range(4):
            slot = offsets[d] + cols_ref[1 + d, b]
            share_ref[slot] += part[:, d * block : (d + 1) * block]
    for at, out_ref in enumerate(outs):
        for s in range(halo):
            start = halo * channels + s * row_regions
            out_ref[start : start + row_regions, :] = share_ref[at * halo + s].astype(BF16)
    for copy in copies[7 + len(parts) :]:
        copy.wait()


def own_terms(
    cols_ref, state_ref, tangent_ref, coef_ref, rate_ref, coupling_ref, acc_ref, own_ref, block, ready=lambda: None
):
    blocks, entries = coef_ref.shape[:2]
    own_ref[blocks] = jnp.zeros(own_ref.shape[1:], BF16)
    high, low = split2(coupling_ref[...] * step_length)
    zero = jnp.zeros_like(high)
    mix_high = jnp.concatenate(
        [jnp.concatenate([high, zero], axis=1), jnp.concatenate([zero, high], axis=1)], axis=0
    )
    mix_low = jnp.concatenate(
        [jnp.concatenate([low, zero], axis=1), jnp.concatenate([zero, low], axis=1)], axis=0
    )
    mix = jnp.concatenate([mix_high, mix_high, mix_low], axis=1)
    for b in range(blocks):
        lanes = slice(b * block, (b + 1) * block)
        state = state_ref[:, lanes]
        tangent = tangent_ref[:, lanes]
        rate = rate_ref[:, lanes]
        squared = state * state
        inverse = 1.0 / (1.0 + squared)
        scaled = rate * inverse
        uptake = scaled * state
        slope = scaled * inverse * (1.0 - squared) * tangent
        term_high, term_low = split2(jnp.concatenate([uptake, slope], axis=0))
        terms = jnp.concatenate([term_high, term_low, term_high], axis=0)
        stacked = jnp.concatenate([state, tangent], axis=0)
        own_ref[b] = stacked.astype(BF16)
        acc_ref[:, lanes] = stacked + jnp.dot(mix, terms, preferred_element_type=F32)
    ready()
    for b in range(blocks):
        lanes = slice(b * block, (b + 1) * block)
        total = acc_ref[:, lanes] + jnp.dot(own_ref[b], coef_ref[b, 0], preferred_element_type=F32)
        for k in range(1, entries):
            index = jnp.minimum(cols_ref[k + 4, b], blocks)
            total += jnp.dot(own_ref[index], coef_ref[b, k], preferred_element_type=F32)
        acc_ref[:, lanes] = total


def own_kernel(
    cols_ref, state_ref, tangent_ref, rate_ref, coupling_ref, coef_hbm, acc_ref, coef_ref, own_ref, sems, *, block
):
    extra = coef_ref.shape[1] - 1
    copies = start_copies(
        [coef_hbm.at[:, 0:1], coef_hbm.at[:, 5 : 5 + extra]], [coef_ref.at[:, 0:1], coef_ref.at[:, 1:]], sems
    )

    def ready():
        for copy in copies:
            copy.wait()

    own_terms(
        cols_ref, state_ref, tangent_ref, coef_ref, rate_ref, coupling_ref, acc_ref, own_ref, block, ready
    )


def slot_offsets(meta_ref, blocks, halo):
    lat_odd = meta_ref[0] % 2
    lon_odd = meta_ref[1] % 2
    shifts = (1 - lat_odd, lat_odd, 3 - lon_odd, 2 + lon_odd)
    return [shifts[d] * halo - (blocks + d * halo) for d in range(4)]


def halo_blocks(meta_ref, recvs, halo_ref, halo):
    channels = halo_ref.shape[1]
    for at, recv in enumerate(recvs):
        for s in range(halo):
            piece = recv[s * channels : (s + 1) * channels, :]
            if at == 1:
                piece = jnp.where(meta_ref[2] > 0, jnp.zeros_like(piece), piece)
            halo_ref[at * halo + s] = piece


def transported(cols_ref, meta_ref, acc_ref, coef_ref, halo_ref, explicit_ref, halo, block):
    blocks = coef_ref.shape[0]
    offsets = slot_offsets(meta_ref, blocks, halo)
    for b in range(blocks):
        pieces = [halo_ref[offsets[d] + cols_ref[1 + d, b]] for d in range(4)]
        gathered = jnp.concatenate(pieces, axis=1)
        weights = coef_ref[b].reshape(4 * block, block)
        moved = jnp.dot(gathered, weights, preferred_element_type=F32)
        explicit_ref[b] = (acc_ref[:, b * block : (b + 1) * block] + moved).astype(BF16)


def step_kernel(
    cols_ref, meta_ref, sends_ref, acc_ref, a_ref, b_ref, c_ref, r_ref, coef_ref, inner_ref, implicit_ref, rate_ref,
    coupling_ref, start_ref, region_ref, m_ref,
    a_out, b_out, c_out, r_out, next_ref, totals_ref, halo_ref, explicit_ref, own_ref, state_ref, tangent_ref, both_ref,
    *, halo, block, row_regions,
):
    recvs = (a_ref, b_ref, c_ref, r_ref)
    outs = (a_out, b_out, c_out, r_out)
    halo_blocks(meta_ref, recvs, halo_ref, halo)
    tracers, rows = state_ref.shape
    channels = 2 * tracers
    blocks = coef_ref.shape[0]
    transported(cols_ref, meta_ref, acc_ref, coef_ref, halo_ref, explicit_ref, halo, block)
    for b in range(blocks):
        lanes = slice(b * block, (b + 1) * block)
        new = jnp.dot(explicit_ref[b], implicit_ref[b], preferred_element_type=F32)
        state_ref[:, lanes] = new[:tracers]
        tangent_ref[:, lanes] = new[tracers:]
        own_ref[b] = new.astype(BF16)
    pick_sends(sends_ref, meta_ref, lambda index: own_ref[index], outs, halo)
    own_terms(cols_ref, state_ref, tangent_ref, inner_ref, rate_ref, coupling_ref, next_ref, own_ref, block)

    nt = (((1,), (1,)), ((), ()))
    high, low = split2(next_ref[tracers:, :])
    both_ref[:tracers, :] = high
    both_ref[tracers:, :] = low
    m_high = m_ref[:row_regions, :]
    sums = lax.dot_general(both_ref[...], m_high, nt, preferred_element_type=F32)
    sums = sums[:tracers] + sums[tracers:]
    sums += lax.dot_general(high, m_ref[row_regions:, :], nt, preferred_element_type=F32)
    ids = lax.broadcasted_iota(jnp.int32, (row_regions, rows), 0) + meta_ref[0] * row_regions
    chosen = (ids == region_ref[...]).astype(F32).astype(BF16)
    high, low = split2(start_ref[...])
    both_ref[:tracers, :] = high
    both_ref[tracers:, :] = low
    begun = lax.dot_general(both_ref[...], chosen, nt, preferred_element_type=F32)
    sums -= begun[:tracers] + begun[tracers:]

    shares = []
    for at in range(4):
        share = jnp.zeros((tracers, row_regions), F32)
        for s in range(halo):
            piece = outs[at][s * channels + tracers : (s + 1) * channels, :]
            start = halo * channels + s * row_regions
            weights = recvs[at][start : start + row_regions, :]
            share += lax.dot_general(piece, weights, nt, preferred_element_type=F32)
        shares.append(share)
    odd = meta_ref[0] % 2 > 0
    none = jnp.zeros((tracers, row_regions), F32)
    shares[1] = jnp.where(meta_ref[2] > 0, none, shares[1])
    here = sums + shares[2] + shares[3]
    total = jnp.concatenate(
        [
            jnp.where(odd, none, shares[1]),
            jnp.where(odd, shares[0], here),
            jnp.where(odd, here, shares[0]),
            jnp.where(odd, shares[1], none),
        ],
        axis=1,
    )
    for at in range(4 * row_regions // block):
        totals_ref[at * tracers : (at + 1) * tracers, :] = total[:, at * block : (at + 1) * block]


def last_kernel(
    cols_ref, meta_ref, acc_ref, a_ref, b_ref, c_ref, r_ref, coef_ref, implicit_ref, start_ref,
    state_hbm, residual_ref, halo_ref, explicit_ref, state_ref, sems, *, halo, block, chunk,
):
    halo_blocks(meta_ref, (a_ref, b_ref, c_ref, r_ref), halo_ref, halo)
    tracers, rows = state_ref.shape
    blocks = coef_ref.shape[0]
    transported(cols_ref, meta_ref, acc_ref, coef_ref, halo_ref, explicit_ref, halo, block)
    copies = []
    for b in range(blocks):
        lanes = slice(b * block, (b + 1) * block)
        new = jnp.dot(explicit_ref[b], implicit_ref[b], preferred_element_type=F32)
        state_ref[:, lanes] = new[:tracers]
        residual_ref[:, lanes] = new[tracers:] - start_ref[:, lanes]
        if (b + 1) % chunk == 0 or b + 1 == blocks:
            part = slice(b // chunk * chunk * block, (b + 1) * block)
            copies += start_copies([state_ref.at[:, part]], [state_hbm.at[:, part]], sems, b // chunk)
    for copy in copies:
        copy.wait()


def prepare_kernel(
    meta_ref, inverse_ref, c_ref, r_ref, region_ref, high_ref, low_ref, chosen_ref, *, skip, block
):
    regions, width = inverse_ref.shape
    for at in range(width // block):
        lanes = slice(at * block, (at + 1) * block)
        rows = slice(skip + at * 2 * regions, skip + (at + 1) * 2 * regions)
        own_high, own_low = split2(inverse_ref[:, lanes])
        c_all = c_ref[rows, :].astype(F32)
        r_all = r_ref[rows, :].astype(F32)
        high_ref[:, lanes] = jnp.concatenate(
            [own_high.astype(F32), c_all[:regions], r_all[:regions]], axis=0
        ).astype(BF16)
        low_ref[:, lanes] = jnp.concatenate(
            [own_low.astype(F32), c_all[regions:], r_all[regions:]], axis=0
        ).astype(BF16)
    rows_id = lax.broadcasted_iota(jnp.int32, (3 * regions, 1), 0)
    group = rows_id // regions
    base = jnp.where(group == 0, meta_ref[3], jnp.where(group == 1, meta_ref[4], meta_ref[5]))
    ids = base * regions + rows_id % regions
    one_hot = (ids == region_ref[...]).astype(F32)
    chosen_ref[...] = jnp.concatenate([one_hot, one_hot], axis=0).astype(BF16)


def correct_kernel(
    meta_ref, stack_ref, high_ref, low_ref, chosen_ref, residual_ref, out_ref, *, row_regions, block
):
    width = high_ref.shape[1]
    tracers = residual_ref.shape[0]
    span = 4 * row_regions
    lines = tracers * span // block
    pair = meta_ref[0] // 2
    total = jnp.zeros((tracers, width), F32)
    for at in range(stack_ref.shape[0] // lines):
        first = at * lines
        value = jnp.concatenate(
            [stack_ref[first + k * tracers : first + (k + 1) * tracers, :] for k in range(span // block)], axis=1
        )
        if width > span:
            value = jnp.concatenate([value, jnp.zeros((tracers, width - span), F32)], axis=1)
        shift = (2 * (pair ^ at) - 1) * row_regions + width
        total += pltpu.roll(value, shift % width, 1)
    t_high, t_low = split2(total)
    both = jnp.concatenate([t_high, t_low], axis=0)
    nt = (((1,), (1,)), ((), ()))
    part = lax.dot_general(both, high_ref[...], nt, preferred_element_type=F32)
    values = part[:tracers] + part[tracers:]
    values += lax.dot_general(t_high, low_ref[...], nt, preferred_element_type=F32)
    v_high = values.astype(BF16).astype(F32)
    pieces = jnp.concatenate([v_high, values - v_high], axis=1).astype(BF16)
    out_ref[...] = residual_ref[...] + jnp.dot(pieces, chosen_ref[...], preferred_element_type=F32)


def partners(n_lat, n_lon):
    def flat(la, lo):
        return la * n_lon + lo

    lat_even, lat_odd, core, ring = [], [], [], []
    for la in range(n_lat):
        for lo in range(n_lon):
            me = flat(la, lo)
            lat_even.append((me, flat(la ^ 1, lo)))
            if la in (0, n_lat - 1):
                lat_odd.append((me, flat(la, lo ^ 1)))
            else:
                lat_odd.append((me, flat(la + 1 if la % 2 else la - 1, lo)))
            core.append((me, flat(la, lo ^ 1)))
            ring.append((me, flat(la, (lo + 1 if lo % 2 else lo - 1) % n_lon)))
    return lat_even, lat_odd, core, ring


def local(
    state_init, tangent_init, coef_blocks, column_lists, send_lists, implicit_blocks,
    uptake_rate, coupling, region_map, coarse_inverse,
):
    n_lat, n_lon = lax.axis_size("lat"), lax.axis_size("lon")
    tracers, rows = state_init.shape
    blocks, entries, block = coef_blocks.shape[:3]
    halo = send_lists.shape[2]
    channels = 2 * tracers
    regions, width = coarse_inverse.shape
    devices = n_lat * n_lon
    lat_pos, lon_pos = lax.axis_index("lat"), lax.axis_index("lon")
    edge = ((lat_pos == 0) | (lat_pos == n_lat - 1)).astype(jnp.int32)
    ring_lon = (lon_pos + jnp.where(lon_pos % 2 == 0, n_lon - 1, 1)) % n_lon
    base = lat_pos * n_lon
    meta = jnp.stack([lat_pos, lon_pos, edge, base + lon_pos, base + (lon_pos ^ 1), base + ring_lon])
    meta = meta.astype(jnp.int32)
    sends = send_lists[0].T
    cols = column_lists.T
    rate = uptake_rate.reshape(1, rows)
    region = region_map.reshape(1, rows)
    perms = partners(n_lat, n_lon)
    row_regions = n_lon * regions
    shared = halo * (channels + row_regions)
    lat_shape = jax.ShapeDtypeStruct((shared, block), BF16)
    lon_shape = jax.ShapeDtypeStruct((shared + 2 * regions * (width // block), block), BF16)
    halo_shape = jax.ShapeDtypeStruct((halo * channels, block), BF16)
    lines = tracers * (4 * row_regions // block)
    totals_shape = jax.ShapeDtypeStruct((lines, block), F32)
    field = jax.ShapeDtypeStruct((tracers, rows), F32)
    acc_shape = jax.ShapeDtypeStruct((channels, rows), F32)
    like = lambda value: jax.ShapeDtypeStruct(value.shape, value.dtype)
    halo_scratch = pltpu.VMEM((4 * halo, channels, block), BF16)
    block_scratch = pltpu.VMEM((blocks, channels, block), BF16)
    own_scratch = pltpu.VMEM((blocks + 1, channels, block), BF16)
    field_scratch = pltpu.VMEM((tracers, rows), F32)
    dma = pltpu.SemaphoreType.DMA
    chunk = 8

    def call(kernel, name, outs, n_smem, n_vmem, n_any, scratch, flops=0, out_specs=None, **static):
        return pl.pallas_call(
            functools.partial(kernel, block=block, **static),
            out_shape=outs,
            in_specs=smem(n_smem) + vmem(n_vmem) + [pl.BlockSpec(memory_space=pltpu.HBM)] * n_any,
            out_specs=jax.tree.map(lambda _: vmem(1)[0], outs) if out_specs is None else out_specs,
            scratch_shapes=scratch,
            compiler_params=params(),
            cost_estimate=pl.CostEstimate(flops=flops, bytes_accessed=10**6, transcendentals=0),
            name=name,
        )

    far = lambda value: pltpu.with_memory_space_constraint(value, pltpu.HBM)
    smalls = (state_init, tangent_init, coarse_inverse, cols, rate, coupling, region)
    prelude = call(
        prelude_kernel, "prelude",
        (lat_shape, lat_shape, lon_shape, lon_shape)
        + tuple(like(v) for v in smalls + (sends,))
        + (jax.ShapeDtypeStruct((blocks, 4, block, block), BF16), like(implicit_blocks))
        + (jax.ShapeDtypeStruct((2 * row_regions, rows), BF16),),
        1, 0, 10,
        [
            pltpu.SMEM(sends.shape, jnp.int32),
            pltpu.SMEM(cols.shape, jnp.int32),
            pltpu.VMEM((4 * halo, row_regions, block), F32),
            dma((11 + -(-blocks // chunk),)),
        ],
        halo=halo, row_regions=row_regions, chunk=chunk,
    )
    inner_shape = jax.ShapeDtypeStruct((blocks, entries - 4, block, block), BF16)
    own = call(own_kernel, "own", (acc_shape, inner_shape), 1, 4, 1, [own_scratch, dma((2,))], flops=10**9)
    step = call(
        step_kernel, "step", (halo_shape,) * 4 + (acc_shape, totals_shape), 3, 13, 0,
        [halo_scratch, block_scratch, own_scratch, field_scratch, field_scratch, pltpu.VMEM((channels, rows), BF16)],
        halo=halo, row_regions=row_regions,
    )
    last = call(
        last_kernel, "last", (field, field), 2, 8, 0,
        [halo_scratch, block_scratch, field_scratch, dma((-(-blocks // chunk),))],
        flops=10**9, out_specs=(pl.BlockSpec(memory_space=pltpu.HBM), vmem(1)[0]), halo=halo, chunk=chunk,
    )
    rows_of = jax.ShapeDtypeStruct((3 * regions, width), BF16)
    prepare = call(
        prepare_kernel, "prepare", (rows_of, rows_of, jax.ShapeDtypeStruct((6 * regions, rows), BF16)), 1, 4, 0, [],
        flops=10**8, skip=shared,
    )
    correct = call(correct_kernel, "correct", field, 1, 5, 0, [], row_regions=row_regions)

    *sent, state, start, inverse, cols, rate, coupling, region, sends, coef, implicit, folded = prelude(
        meta, *map(far, (sends, *smalls, coef_blocks, implicit_blocks))
    )
    got1 = [lax.ppermute(value, BOTH, pairs) for value, pairs in zip(sent, perms)]
    acc, inner = own(cols, state, start, rate, coupling, far(coef_blocks))
    *sent, acc, totals = step(
        cols, meta, sends, acc, *got1, coef, inner, implicit, rate, coupling, start, region, folded
    )
    got2 = [None] * 4
    height = halo * channels

    def swap(mask):
        return [(i, i ^ mask) for i in range(devices)]

    def loaded(at, value):
        high = lax.reduce_precision(value, 8, 7)
        return jnp.concatenate([sent[at], high.astype(BF16), (value - high).astype(BF16)], axis=0)

    def share_of(at):
        more = got2[at][height:].astype(F32)
        return more[:lines] + more[lines:]

    bit = 1
    while bit < devices:
        if bit > n_lon:
            if got2[1] is None:
                totals, sent[1] = lax.optimization_barrier((totals, sent[1]))
                got2[1] = lax.ppermute(sent[1], BOTH, perms[1])
            totals = jnp.concatenate([totals, lax.ppermute(totals, BOTH, swap(bit | 1))], axis=0)
        elif bit == 2 and n_lon == 4 and perms[3] == swap(3) and perms[0] == swap(4):
            for at in (3, 0):
                got2[at] = lax.ppermute(loaded(at, totals), BOTH, perms[at])
            across = lax.ppermute(totals, BOTH, swap(7))
            totals = totals + share_of(3) + share_of(0) + across
            bit = 4
        else:
            matches = [(at, swap(mask)) for mask in (bit | 1, bit) for at in range(4) if perms[at] == swap(mask)]
            if matches:
                at, pairs = matches[0]
                got2[at] = lax.ppermute(loaded(at, totals), BOTH, pairs)
                totals = totals + share_of(at)
            else:
                totals = totals + lax.ppermute(totals, BOTH, swap(bit | 1))
        bit *= 2
    for at in range(4):
        if got2[at] is None:
            got2[at] = lax.ppermute(sent[at], BOTH, perms[at])
    final_state, residual = last(cols, meta, acc, *got2, coef, implicit, start)
    preconditioned = correct(meta, totals, *prepare(meta, inverse, got1[2], got1[3], region), residual)
    return final_state, preconditioned


def solution(mesh):
    placed = (
        P(None, BOTH),
        P(None, BOTH),
        P(BOTH, None, None, None),
        P(BOTH, None),
        P(BOTH, None, None),
        P(BOTH, None, None),
        P(BOTH),
        P(),
        P(BOTH),
        P(BOTH, None),
    )
    return jax.shard_map(
        local,
        mesh=mesh,
        in_specs=placed,
        out_specs=(P(None, BOTH), P(None, BOTH)),
        check_vma=False,
    )
```
